32 devices in a mesh: groups: 2 (over y), row: 16 (over z, x, core).
Axes of the slice: x: 2, y: 2, z: 4, core: 2. Of those that a mesh axis runs over, the one named last changes fastest.
Arguments:
- late_grads: bfloat16 [64, 16, 4, 4096], P(('groups', 'row')), parts along dimension 0, may hold values from -6 to 6
- projections: bfloat16 [4096, 256], replicated, may hold values from -0.09375 to 0.09375
- recent_sketches: bfloat16 [8192, 8192], P(('groups', 'row')), parts along dimension 0, may hold values from -6 to 6
Outputs:
- reweighted: bfloat16 [64, 8192], P(('groups', 'row')), parts along dimension 0
The draws below stay inside these ranges and needn't reach their ends.
There are 2 independent parts, one for each index of `groups`. The reference program is written for one: setup_inputs(seed, part) draws one part's arguments, and reference() takes and returns one part's arrays. A program takes and returns all parts, laid end to end along the dimension named above; an argument that names none is the same for every part. Nothing has to cross between parts.
All inputs are finite; a program needn't handle non-finite values.
Results may differ from the reference program's by a relative error of at most 0.0076.
Values may be sent and summed in bfloat16 or wider, within the bound.
A program may use at most 64 MiB of HBM per device.

```python
import jax
import jax.numpy as jnp

D = 4096
RANK = 64
ITEMS = 16
K = 8192
L_TOT = 32
R_TOT = 4096


def steps_of(key, shape, pieces, smallest, largest):
    def one(position, blocks):
        draws = jax.random.uniform(jax.random.fold_in(jax.random.fold_in(key, 6), position), (blocks,), jnp.float32, smallest / len(pieces), largest / len(pieces))
        return jnp.repeat(jnp.exp(draws), shape[position] // blocks).reshape((-1,) + (1,) * (len(shape) - position - 1))

    gain = one(*pieces[0])
    for cut in pieces[1:]:
        gain = gain * one(*cut)
    return gain


def bell_draw(own_key, shape, width, bound, cuts=(), held_as=jnp.bfloat16):
    array = width * jax.random.normal(own_key, shape, jnp.float32)
    if cuts:
        array = array * steps_of(own_key, shape, cuts, -0.22, 0.18)
    return jnp.clip(array, -bound, bound).astype(held_as)


def setup_inputs(seed: int = 0, part: int = 0) -> dict:
    seeds = jax.random.split(jax.random.key(seed), 4)
    part_splits = jax.random.split(jax.random.fold_in(seeds[3], part), 4)
    late_grads = bell_draw(part_splits[0], (L_TOT, ITEMS, 4, D), 1.0, 6.0, ((0, 16),))
    projections = bell_draw(seeds[1], (D, 4 * RANK), D ** -0.5, 0.09375)
    recent_sketches = bell_draw(part_splits[2], (R_TOT, K), 1.0, 6.0, ((0, 16),))
    return dict(late_grads=late_grads, projections=projections, recent_sketches=recent_sketches)


def build_sketch(factors):
    count = factors.shape[0]
    parts = factors.reshape(count, ITEMS, 4, RANK)
    blocks = []
    for layer in range(2):
        left = parts[:, :, 2 * layer + 1, :].astype(jnp.float32)
        right = parts[:, :, 2 * layer, :].astype(jnp.float32)
        outer = jnp.einsum('eti,etj->eij', left, right)
        blocks.append(outer.reshape(count, RANK * RANK))
    joined = jnp.concatenate(blocks, axis=1) / jnp.sqrt(jnp.float32(ITEMS))
    return joined.astype(jnp.bfloat16)

def reference(late_grads, projections, recent_sketches):
    proj_blocks = projections.reshape(D, 4, RANK).astype(jnp.float32)
    factors = jnp.einsum('etkd,dkr->etkr', late_grads.astype(jnp.float32), proj_blocks)
    factors = factors.astype(jnp.bfloat16).reshape(L_TOT, ITEMS, 4 * RANK)
    late_sketch = build_sketch(factors)
    similarity = jnp.dot(late_sketch, recent_sketches.T, preferred_element_type=jnp.float32) / jnp.sqrt(jnp.float32(K))
    weights = jnp.tanh(similarity).astype(jnp.bfloat16)
    summed = jnp.dot(weights, recent_sketches, preferred_element_type=jnp.float32)
    return (summed / jnp.sqrt(jnp.float32(R_TOT))).astype(jnp.bfloat16)
```

```python
import functools
import math

import jax
import jax.numpy as jnp
from jax import lax
from jax.experimental import pallas as pl
from jax.experimental.pallas import tpu as pltpu
from jax.sharding import PartitionSpec as P

GROUP = 8
CHUNKS = 2
LOADS = 4
BLOCK = 32
LANES = 128
MESH = pl.DeviceIdType.MESH


def kernel(
    dims, items, rank, total_recent,
    late_hbm, proj_hbm, recent_hbm, out_ref,
    late, proj, recent, fac, other, mysim, itssim, tf, tb, land,
    load_sem, f_send, f_recv, r_send, r_recv, s_send, s_recv, m_send, m_recv,
):
    nz, nx, nc = dims
    n = nz * nx * nc
    local_recent = recent_hbm.shape[0]
    half = recent.shape[1]
    width = recent_hbm.shape[1]
    chips, pairs, pair_lanes = nz * nx, fac.shape[1], fac.shape[2]
    examples = pairs // items
    slab = examples * GROUP
    gw = half // GROUP
    cw = gw // CHUNKS
    bf16, f32 = jnp.bfloat16, jnp.float32
    me = lax.axis_index("row")
    mc = lax.rem(me, nc)
    mx = lax.rem(lax.div(me, nc), nx)
    mz = lax.div(me, nc * nx)
    oc = 1 - mc

    def across(z, d):
        bit = 1
        while bit <= d:
            if d & bit:
                z = z + bit - 2 * bit * lax.rem(lax.div(z, bit), 2)
            bit *= 2
        return z

    peers = []
    for dz in reversed(range(nz)):
        for dx in reversed(range(nx)):
            for dc in (1, 0):
                if dz or dx or dc:
                    z, x = across(mz, dz), lax.rem(mx + dx, nx)
                    c = oc if dc else mc
                    peers.append(((z * nx + x) * nc + c, dc))
    partner = (mz * nx + mx) * nc + oc

    depth = late.shape[2] // LOADS
    load_inputs = []
    for i in range(LOADS):
        part_of = pl.ds(i * depth, depth)
        pair = (
            pltpu.make_async_copy(late_hbm.at[:, :, part_of], late.at[:, :, part_of], load_sem.at[1 + i]),
            pltpu.make_async_copy(proj_hbm.at[part_of], proj.at[part_of], load_sem.at[1 + LOADS + i]),
        )
        for copy in pair:
            copy.start()
        load_inputs.append(pair)

    own_rows = pl.ds(pl.multiple_of(mc * local_recent, local_recent), local_recent)
    its_rows = pl.ds(pl.multiple_of(oc * local_recent, local_recent), local_recent)
    own_half = pl.ds(pl.multiple_of(mc * half, half), half)
    its_half = pl.ds(pl.multiple_of(oc * half, half), half)
    load_recent = pltpu.make_async_copy(
        recent_hbm.at[:, own_half], recent.at[own_rows, :], load_sem.at[0]
    )
    load_recent.start()

    barrier = pltpu.get_barrier_semaphore()
    for index, _ in peers:
        pl.semaphore_signal(barrier, inc=1, device_id={"row": index}, device_id_type=MESH)

    def where(shape, expr):
        r = lax.broadcasted_iota(jnp.int32, shape, 0)
        c = lax.broadcasted_iota(jnp.int32, shape, 1)
        return expr(r, c)

    def onehot(shape, expr):
        return jnp.where(where(shape, expr), 1.0, 0.0).astype(bf16)

    pick = onehot((pairs, 4 * pairs), lambda r, c: r == lax.shift_right_logical(c, 2))
    full = jnp.zeros((4 * pairs, 4 * rank), f32)
    for i, pair in enumerate(load_inputs):
        for copy in pair:
            copy.wait()
        rows = late[:, :, i * depth : (i + 1) * depth].reshape(4 * pairs, depth)
        full = full + jnp.dot(rows, proj[i * depth : (i + 1) * depth, :], preferred_element_type=f32)
    full = jnp.where(
        where(full.shape, lambda r, c: lax.rem(r, 4) == lax.div(c, rank)), full, 0.0
    ).astype(bf16)
    factors = jnp.dot(pick, full, preferred_element_type=f32)
    first, second = factors[:, :pair_lanes], factors[:, pair_lanes:]
    fac[me] = jnp.where(mc == 0, first, second).astype(bf16)
    other[...] = jnp.where(mc == 0, second, first).astype(bf16)

    pl.semaphore_wait(barrier, n - 1)

    sent = []

    def start(src, dst, ss, rs, to):
        copy = pltpu.make_async_remote_copy(
            src_ref=src, dst_ref=dst, send_sem=ss, recv_sem=rs,
            device_id={"row": to}, device_id_type=MESH,
        )
        copy.start()
        sent.append(copy)
        return copy

    for slot, (to, dc) in enumerate(peers):
        start(other if dc else fac.at[me], fac.at[me], f_send.at[slot], f_recv.at[me], to)
    its_recent = start(
        recent_hbm.at[:, its_half], recent.at[own_rows, :], r_send.at[0], r_recv.at[0], partner
    )
    for source, _ in peers:
        pltpu.make_async_remote_copy(
            src_ref=other, dst_ref=fac.at[source], send_sem=f_send.at[0], recv_sem=f_recv.at[source],
            device_id={"row": partner}, device_id_type=MESH,
        ).wait_recv()

    rows = BLOCK * items
    lanes = GROUP * items
    quad = 4
    many = rank // quad
    lift = onehot(
        (rank * GROUP, pair_lanes),
        lambda r, c: c == rank + quad * lax.div(lax.rem(r, many * GROUP), GROUP) + lax.div(r, many * GROUP),
    )
    twice = onehot((pair_lanes, 2 * rank), lambda r, c: r == lax.rem(c, rank))
    same = where(
        (rank * GROUP, rows), lambda r, c: lax.rem(r, GROUP) == lax.rem(lax.div(c, items), GROUP)
    )
    left_half = where((many * GROUP, 2 * rank), lambda r, c: c < rank)

    blocks = n * pairs // rows

    def each_block(body):
        if blocks == 1:
            body(0)
        else:
            lax.fori_loop(0, blocks, lambda b, c: (body(b), c)[1], 0)

    def similar(b):
        per = rows // pairs
        every = fac[pl.ds(b * per, per)].reshape(rows, pair_lanes)
        lifted = lax.dot_general(lift, every, (((1,), (1,)), ((), ())), preferred_element_type=f32)
        lifted = jnp.where(same, lifted, 0.0).astype(bf16)
        right = jnp.dot(every, twice, preferred_element_type=f32).astype(bf16)
        tall = many * GROUP
        wide = []
        for g in range(rows // lanes):
            outer = jnp.dot(
                lifted[:, g * lanes : (g + 1) * lanes], right[g * lanes : (g + 1) * lanes, :],
                preferred_element_type=f32,
            )
            low = jnp.where(left_half, outer[:tall], outer[tall : 2 * tall])
            high = jnp.where(left_half, outer[2 * tall : 3 * tall], outer[3 * tall :])
            wide.append((low, high))
        pieces = []
        for a in range(many):
            for side in range(2):
                pieces.append(jnp.concatenate([w[side][a * GROUP : (a + 1) * GROUP] for w in wide], axis=0))
        return (jnp.concatenate(pieces, axis=1) * (1.0 / math.sqrt(items))).astype(bf16)

    at = lambda b: pl.ds(b * BLOCK, BLOCK)
    contract = (((1,), (1,)), ((), ()))

    def partial(b):
        sketch = similar(b)
        mysim[mc, at(b)] = lax.dot_general(sketch, recent[own_rows, :], contract, preferred_element_type=f32)
        if blocks == 1:
            copies.append(start(mysim.at[mc], itssim.at[mc], s_send.at[0], s_recv.at[0], partner))
            its_recent.wait_recv()
        mysim[oc, at(b)] = lax.dot_general(sketch, recent[its_rows, :], contract, preferred_element_type=f32)
        if blocks == 1:
            copies.append(start(mysim.at[oc], itssim.at[oc], s_send.at[1], s_recv.at[1], partner))

    copies = []
    load_recent.wait()
    if blocks > 1:
        its_recent.wait_recv()
    each_block(partial)
    if blocks > 1:
        copies.append(start(mysim, itssim, s_send.at[0], s_recv.at[0], partner))
    if blocks == 1:
        pltpu.make_async_remote_copy(
            src_ref=mysim.at[oc], dst_ref=itssim.at[oc], send_sem=s_send.at[0], recv_sem=s_recv.at[0],
            device_id={"row": partner}, device_id_type=MESH,
        ).wait_recv()
        pltpu.make_async_remote_copy(
            src_ref=mysim.at[mc], dst_ref=itssim.at[mc], send_sem=s_send.at[1], recv_sem=s_recv.at[1],
            device_id={"row": partner}, device_id_type=MESH,
        ).wait_recv()
    else:
        copies[0].wait_recv()

    def term(b, k):
        sims = jnp.concatenate(
            [mysim[h, at(b)] + itssim[h, at(b)] for h in range(nc)], axis=1
        ) * (1.0 / math.sqrt(width))
        weights = jnp.tanh(sims).astype(bf16)
        for g in range(GROUP):
            lo = g * gw + k * cw
            got = jnp.dot(weights, recent[:, lo : lo + cw], preferred_element_type=f32)
            for j in range(cw // LANES):
                tf[k, j, pl.ds(b * BLOCK * GROUP + g, BLOCK, stride=GROUP), :] = got[
                    :, j * LANES : (j + 1) * LANES
                ]
        here = pl.ds(b * BLOCK * GROUP, BLOCK * GROUP)
        for j in range(cw // LANES):
            tb.at[k].reshape(n * slab, cw)[here, j * LANES : (j + 1) * LANES] = tf[k, j, here].astype(bf16)

    for k in range(CHUNKS):
        each_block(functools.partial(term, k=k))
        for slot, (to, _) in enumerate(peers):
            start(tb.at[k, to], land.at[k, me], m_send.at[k, slot], m_recv.at[k, me], to)
        land[k, me] = tb[k, me]

    for k in range(CHUNKS):
        for source, _ in reversed(peers):
            pltpu.make_async_remote_copy(
                src_ref=tb.at[k, 0], dst_ref=land.at[k, source], send_sem=m_send.at[k, 0],
                recv_sem=m_recv.at[k, source], device_id={"row": partner}, device_id_type=MESH,
            ).wait_recv()
        totals = []
        for c in range(nc):
            total = land[k, c].astype(f32)
            for q in range(1, chips):
                total = total + land[k, q * nc + c].astype(f32)
            totals.append(total)
        rows_out = [
            t[e * GROUP : (e + 1) * GROUP] for e in range(examples) for t in totals
        ]
        out_ref[:, k * cw : (k + 1) * cw] = (
            jnp.concatenate(rows_out, axis=0) * (1.0 / math.sqrt(total_recent))
        ).astype(bf16)
    for copy in sent:
        copy.wait_send()


def per_device(dims, late_grads, projections, recent_sketches):
    nz, nx, nc = dims
    local_rows, items, kinds, width_in = late_grads.shape
    rank = projections.shape[1] // 4
    local_recent, width = recent_sketches.shape
    n = nz * nx * nc
    half = width // 2
    slab, cw = local_rows * GROUP, half // GROUP // CHUNKS
    every = n * local_rows
    bf16, f32 = jnp.bfloat16, jnp.float32
    dma = pltpu.SemaphoreType.DMA
    out = pl.pallas_call(
        functools.partial(kernel, dims, items, rank, local_recent * n),
        out_shape=pltpu.VMEM((2 * slab, half // GROUP), bf16),
        in_specs=[pl.BlockSpec(memory_space=pl.ANY)] * 3,
        out_specs=pl.BlockSpec(memory_space=pltpu.VMEM),
        scratch_shapes=[
            pltpu.VMEM((local_rows * items, kinds, width_in), bf16),
            pltpu.VMEM(projections.shape, bf16),
            pltpu.VMEM((nc * local_recent, half), bf16),
            pltpu.VMEM((n, local_rows * items, 2 * rank), bf16),
            pltpu.VMEM((local_rows * items, 2 * rank), bf16),
            pltpu.VMEM((nc, every, local_recent), f32),
            pltpu.VMEM((nc, every, local_recent), f32),
            pltpu.VMEM((CHUNKS, cw // LANES, every * GROUP, LANES), f32),
            pltpu.VMEM((CHUNKS, n, slab, cw), bf16),
            pltpu.VMEM((CHUNKS, n, slab, cw), bf16),
            dma((1 + 2 * LOADS,)),
            dma((n - 1,)),
            dma((n,)),
            dma((1,)),
            dma((1,)),
            dma((2,)),
            dma((2,)),
            dma((CHUNKS, n - 1)),
            dma((CHUNKS, n)),
        ],
        compiler_params=pltpu.CompilerParams(
            collective_id=0, has_side_effects=True, vmem_limit_bytes=60 * 1024 * 1024
        ),
    )(late_grads.reshape(local_rows * items, kinds, width_in), projections, recent_sketches)
    return out.reshape(local_rows, width)


def solution(mesh):
    n = mesh.shape["row"]
    nx = 4 if n >= 64 else 2
    dims = (n // (2 * nx), nx, 2)
    placed = (P(("groups", "row"), None, None, None), P(), P(("groups", "row"), None))
    return jax.shard_map(
        functools.partial(per_device, dims),
        mesh=mesh,
        in_specs=placed,
        out_specs=P(("groups", "row"), None),
        check_vma=False,
    )
```

```python
import functools
import math

import jax
import jax.numpy as jnp
from jax import lax
from jax.experimental import pallas as pl
from jax.experimental.pallas import tpu as pltpu
from jax.sharding import PartitionSpec as P

GROUP = 8
CHUNKS = 2
LOADS = 4
BLOCK = 32
LANES = 128
MESH = pl.DeviceIdType.MESH


def kernel(
    dims, items, rank, total_recent,
    late_hbm, proj_hbm, recent_hbm, out_ref,
    late, proj, recent, turned, fac, other, mysim, itssim, tf, tb, xland, xb, land,
    load_sem, f_send, f_recv, r_send, r_recv, s_send, s_recv, x_send, x_recv, m_send, m_recv,
):
    nz, nx, nc = dims
    n = nz * nx * nc
    local_recent = recent_hbm.shape[0]
    half = recent.shape[1]
    width = recent_hbm.shape[1]
    pairs, pair_lanes = fac.shape[1:]
    examples = pairs // items
    slab = examples * GROUP
    gw = half // GROUP
    cw = gw // CHUNKS
    bf16, f32 = jnp.bfloat16, jnp.float32
    me = lax.axis_index("row")
    mc = lax.rem(me, nc)
    mx = lax.rem(lax.div(me, nc), nx)
    mz = lax.div(me, nc * nx)
    oc = 1 - mc

    def across(z, d):
        bit = 1
        while bit <= d:
            if d & bit:
                z = z + bit - 2 * bit * lax.rem(lax.div(z, bit), 2)
            bit *= 2
        return z

    peers, places = [], []
    for dz in reversed(range(nz)):
        for dx in reversed(range(nx)):
            for dc in (1, 0):
                if dz or dx or dc:
                    z, x = across(mz, dz), lax.rem(mx + dx, nx)
                    c = oc if dc else mc
                    peers.append(((z * nx + x) * nc + c, dc))
                    places.append((z, x, c, 2 * dz >= nz, dx))
    partner = (mz * nx + mx) * nc + oc

    barrier = pltpu.get_barrier_semaphore()
    for index, _ in peers:
        pl.semaphore_signal(barrier, inc=1, device_id={"row": index}, device_id_type=MESH)

    depth = late.shape[2] // LOADS
    load_inputs = []
    for i in range(LOADS):
        part_of = pl.ds(i * depth, depth)
        pair = (
            pltpu.make_async_copy(late_hbm.at[:, :, part_of], late.at[:, :, part_of], load_sem.at[1 + i]),
            pltpu.make_async_copy(proj_hbm.at[part_of], proj.at[part_of], load_sem.at[1 + LOADS + i]),
        )
        for copy in pair:
            copy.start()
        load_inputs.append(pair)

    own_rows = pl.ds(pl.multiple_of(mc * local_recent, local_recent), local_recent)
    its_rows = pl.ds(pl.multiple_of(oc * local_recent, local_recent), local_recent)
    own_half = pl.ds(pl.multiple_of(mc * half, half), half)
    its_half = pl.ds(pl.multiple_of(oc * half, half), half)
    load_recent = pltpu.make_async_copy(
        recent_hbm.at[:, own_half], recent.at[own_rows, :], load_sem.at[0]
    )
    load_recent.start()

    def where(shape, expr):
        r = lax.broadcasted_iota(jnp.int32, shape, 0)
        c = lax.broadcasted_iota(jnp.int32, shape, 1)
        return expr(r, c)

    def onehot(shape, expr):
        return jnp.where(where(shape, expr), 1.0, 0.0).astype(bf16)

    pick = onehot((pairs, 4 * pairs), lambda r, c: r == lax.shift_right_logical(c, 2))
    full = jnp.zeros((4 * pairs, 4 * rank), f32)
    for i, pair in enumerate(load_inputs):
        for copy in pair:
            copy.wait()
        rows = late[:, :, i * depth : (i + 1) * depth].reshape(4 * pairs, depth)
        full = full + jnp.dot(rows, proj[i * depth : (i + 1) * depth, :], preferred_element_type=f32)
    full = jnp.where(
        where(full.shape, lambda r, c: lax.rem(r, 4) == lax.div(c, rank)), full, 0.0
    ).astype(bf16)
    factors = jnp.dot(pick, full, preferred_element_type=f32)
    first, second = factors[:, :pair_lanes], factors[:, pair_lanes:]
    fac[me] = jnp.where(mc == 0, first, second).astype(bf16)
    other[...] = jnp.where(mc == 0, second, first).astype(bf16)

    pl.semaphore_wait(barrier, n - 1)

    sent = []

    def start(src, dst, ss, rs, to):
        copy = pltpu.make_async_remote_copy(
            src_ref=src, dst_ref=dst, send_sem=ss, recv_sem=rs,
            device_id={"row": to}, device_id_type=MESH,
        )
        copy.start()
        sent.append(copy)
        return copy

    for slot, (to, dc) in enumerate(peers):
        start(other if dc else fac.at[me], fac.at[me], f_send.at[slot], f_recv.at[me], to)
    its_recent = start(
        recent_hbm.at[:, its_half], recent.at[own_rows, :], r_send.at[0], r_recv.at[0], partner
    )
    def turn(rows_at, lanes_at):
        for a in range(0, half, 2 * LANES):
            turned[a : a + 2 * LANES, lanes_at] = recent[rows_at, a : a + 2 * LANES].T

    load_recent.wait()
    turn(own_rows, own_rows)
    its_recent.wait_recv()
    turn(its_rows, its_rows)
    for source, _ in peers:
        pltpu.make_async_remote_copy(
            src_ref=other, dst_ref=fac.at[source], send_sem=f_send.at[0], recv_sem=f_recv.at[source],
            device_id={"row": partner}, device_id_type=MESH,
        ).wait_recv()

    rows = BLOCK * items
    lanes = GROUP * items
    quad = 4
    many = rank // quad
    lift = onehot(
        (rank * GROUP, pair_lanes),
        lambda r, c: c == rank + quad * lax.div(lax.rem(r, many * GROUP), GROUP) + lax.div(r, many * GROUP),
    )
    twice = onehot((pair_lanes, 2 * rank), lambda r, c: r == lax.rem(c, rank))
    same = where(
        (rank * GROUP, rows), lambda r, c: lax.rem(r, GROUP) == lax.rem(lax.div(c, items), GROUP)
    )
    left_half = where((many * GROUP, 2 * rank), lambda r, c: c < rank)

    blocks = n * pairs // rows

    def each_block(body):
        if blocks == 1:
            body(0)
        else:
            lax.fori_loop(0, blocks, lambda b, c: (body(b), c)[1], 0)

    def similar(b):
        per = rows // pairs
        every = fac[pl.ds(b * per, per)].reshape(rows, pair_lanes)
        lifted = lax.dot_general(lift, every, (((1,), (1,)), ((), ())), preferred_element_type=f32)
        lifted = jnp.where(same, lifted, 0.0).astype(bf16)
        right = jnp.dot(every, twice, preferred_element_type=f32).astype(bf16)
        tall = many * GROUP
        wide = []
        for g in range(rows // lanes):
            outer = jnp.dot(
                lifted[:, g * lanes : (g + 1) * lanes], right[g * lanes : (g + 1) * lanes, :],
                preferred_element_type=f32,
            )
            low = jnp.where(left_half, outer[:tall], outer[tall : 2 * tall])
            high = jnp.where(left_half, outer[2 * tall : 3 * tall], outer[3 * tall :])
            wide.append((low, high))
        pieces = []
        for a in range(many):
            for side in range(2):
                pieces.append(jnp.concatenate([w[side][a * GROUP : (a + 1) * GROUP] for w in wide], axis=0))
        return (jnp.concatenate(pieces, axis=1) * (1.0 / math.sqrt(items))).astype(bf16)

    at = lambda b: pl.ds(b * BLOCK, BLOCK)

    def partial(b):
        sketch = similar(b)
        mysim[mc, at(b)] = jnp.dot(sketch, turned[:, own_rows], preferred_element_type=f32)
        if blocks == 1:
            copies.append(start(mysim.at[mc], itssim.at[mc], s_send.at[0], s_recv.at[0], partner))
        mysim[oc, at(b)] = jnp.dot(sketch, turned[:, its_rows], preferred_element_type=f32)
        if blocks == 1:
            copies.append(start(mysim.at[oc], itssim.at[oc], s_send.at[1], s_recv.at[1], partner))

    copies = []
    each_block(partial)
    if blocks > 1:
        copies.append(start(mysim, itssim, s_send.at[0], s_recv.at[0], partner))
    if blocks == 1:
        pltpu.make_async_remote_copy(
            src_ref=mysim.at[oc], dst_ref=itssim.at[oc], send_sem=s_send.at[0], recv_sem=s_recv.at[0],
            device_id={"row": partner}, device_id_type=MESH,
        ).wait_recv()
        pltpu.make_async_remote_copy(
            src_ref=mysim.at[mc], dst_ref=itssim.at[mc], send_sem=s_send.at[1], recv_sem=s_recv.at[1],
            device_id={"row": partner}, device_id_type=MESH,
        ).wait_recv()
    else:
        copies[0].wait_recv()

    def term(b, k):
        sims = jnp.concatenate(
            [mysim[h, at(b)] + itssim[h, at(b)] for h in range(nc)], axis=1
        ) * (1.0 / math.sqrt(width))
        weights = jnp.tanh(sims).astype(bf16)
        for g in range(GROUP):
            lo = g * gw + k * cw
            got = jnp.dot(weights, recent[:, lo : lo + cw], preferred_element_type=f32)
            for j in range(cw // LANES):
                tf[k, j, pl.ds(b * BLOCK * GROUP + g, BLOCK, stride=GROUP), :] = got[
                    :, j * LANES : (j + 1) * LANES
                ]
        tall = nc * slab
        for i in range(BLOCK * GROUP // tall):
            q = b * (BLOCK * GROUP // tall) + i
            z, x = (q // nx, q % nx) if blocks == 1 else (lax.div(q, nx), lax.rem(q, nx))
            for j in range(cw // LANES):
                tb[k, x, z, :, :, j * LANES : (j + 1) * LANES] = (
                    tf[k, j, pl.ds(q * tall, tall)].reshape(nc, slab, LANES).astype(bf16)
                )

    hz = nz // 2
    far_z = (1 - lax.div(mz, hz)) * hz
    near_z = hz - far_z

    def remote(src, dst, ss, rs, to):
        return pltpu.make_async_remote_copy(
            src_ref=src, dst_ref=dst, send_sem=ss, recv_sem=rs,
            device_id={"row": to}, device_id_type=MESH,
        )

    def straight(k, slot):
        z, x, c = places[slot][:3]
        return remote(
            tb.at[k, x, z, c], land.at[k, me], m_send.at[k, slot], m_recv.at[k, me], peers[slot][0]
        )

    def sideways(k, d):
        x = lax.rem(mx + d, nx)
        return remote(
            tb.at[k, x, pl.ds(far_z, hz)], xland.at[k, d - 1], x_send.at[k, d - 1],
            x_recv.at[k, d - 1], (mz * nx + x) * nc + mc,
        )

    def onward(k, slot):
        z, _, c = places[slot][:3]
        return remote(
            xb.at[k, z - far_z, c], land.at[k, me], m_send.at[k, slot], m_recv.at[k, me],
            peers[slot][0],
        )

    slots = range(n - 1)
    far_slots = [i for i in slots if places[i][3]]
    near_slots = [i for i in slots if not places[i][3]]
    column_slots = [i for i in far_slots if not places[i][4]]

    for k in range(CHUNKS):
        each_block(functools.partial(term, k=k))

        @pl.when(mc == 0)
        def _():
            for slot in far_slots + near_slots:
                straight(k, slot).start()

        @pl.when(mc == 1)
        def _():
            for d in range(1, nx):
                sideways(k, d).start()
            for slot in near_slots:
                straight(k, slot).start()

        land[k, me] = tb[k, mx, mz, mc]

    @pl.when(mc == 1)
    def _():
        for k in range(CHUNKS):
            total = tb[k, mx, pl.ds(far_z, hz)].astype(f32)
            for d in range(1, nx):
                sideways(k, d).wait_recv()
                total = total + xland[k, d - 1].astype(f32)
            xb[k] = total.astype(bf16)
            for slot in column_slots:
                onward(k, slot).start()

    def landed(k, source):
        remote(
            tb.at[k, 0, 0, 0], land.at[k, source], m_send.at[k, 0], m_recv.at[k, source], partner
        ).wait_recv()

    def collect(k, places_of, total, c):
        for z, x in places_of:
            total = total + land[k, (z * nx + x) * nc + c].astype(f32)
        return total

    near = [(near_z + z, x) for z in range(hz) for x in range(nx)]
    far = [(far_z + z, x) for z in range(hz) for x in range(nx)]
    column = [(far_z + z, mx) for z in range(hz)]
    for k in range(CHUNKS):
        for slot in reversed(slots):
            z, x, c, is_far, dx = places[slot]
            source = peers[slot][0]
            if is_far and dx:

                @pl.when(c == 0)
                def _():
                    landed(k, source)
            else:
                landed(k, source)
        zero = jnp.zeros((slab, cw), f32)
        totals = [collect(k, near + far, zero, 0), collect(k, near + column, zero, 1)]
        rows_out = [
            t[e * GROUP : (e + 1) * GROUP] for e in range(examples) for t in totals
        ]
        out_ref[:, k * cw : (k + 1) * cw] = (
            jnp.concatenate(rows_out, axis=0) * (1.0 / math.sqrt(total_recent))
        ).astype(bf16)

    for k in range(CHUNKS):

        @pl.when(mc == 0)
        def _():
            for slot in slots:
                straight(k, slot).wait_send()

        @pl.when(mc == 1)
        def _():
            for d in range(1, nx):
                sideways(k, d).wait_send()
            for slot in near_slots:
                straight(k, slot).wait_send()
            for slot in column_slots:
                onward(k, slot).wait_send()

    for copy in sent:
        copy.wait_send()


def per_device(dims, late_grads, projections, recent_sketches):
    nz, nx, nc = dims
    local_rows, items, kinds, width_in = late_grads.shape
    rank = projections.shape[1] // 4
    local_recent, width = recent_sketches.shape
    n = nz * nx * nc
    half = width // 2
    slab, cw = local_rows * GROUP, half // GROUP // CHUNKS
    every = n * local_rows
    bf16, f32 = jnp.bfloat16, jnp.float32
    dma = pltpu.SemaphoreType.DMA
    out = pl.pallas_call(
        functools.partial(kernel, dims, items, rank, local_recent * n),
        out_shape=pltpu.VMEM((2 * slab, half // GROUP), bf16),
        in_specs=[pl.BlockSpec(memory_space=pl.ANY)] * 3,
        out_specs=pl.BlockSpec(memory_space=pltpu.VMEM),
        scratch_shapes=[
            pltpu.VMEM((local_rows * items, kinds, width_in), bf16),
            pltpu.VMEM(projections.shape, bf16),
            pltpu.VMEM((nc * local_recent, half), bf16),
            pltpu.VMEM((half, nc * local_recent), bf16),
            pltpu.VMEM((n, local_rows * items, 2 * rank), bf16),
            pltpu.VMEM((local_rows * items, 2 * rank), bf16),
            pltpu.VMEM((nc, every, local_recent), f32),
            pltpu.VMEM((nc, every, local_recent), f32),
            pltpu.VMEM((CHUNKS, cw // LANES, every * GROUP, LANES), f32),
            pltpu.VMEM((CHUNKS, nx, nz, nc, slab, cw), bf16),
            pltpu.VMEM((CHUNKS, nx - 1, nz // 2, nc, slab, cw), bf16),
            pltpu.VMEM((CHUNKS, nz // 2, nc, slab, cw), bf16),
            pltpu.VMEM((CHUNKS, n, slab, cw), bf16),
            dma((1 + 2 * LOADS,)),
            dma((n - 1,)),
            dma((n,)),
            dma((1,)),
            dma((1,)),
            dma((2,)),
            dma((2,)),
            dma((CHUNKS, nx - 1)),
            dma((CHUNKS, nx - 1)),
            dma((CHUNKS, n - 1)),
            dma((CHUNKS, n)),
        ],
        compiler_params=pltpu.CompilerParams(
            collective_id=0, has_side_effects=True, vmem_limit_bytes=60 * 1024 * 1024
        ),
    )(late_grads.reshape(local_rows * items, kinds, width_in), projections, recent_sketches)
    return out.reshape(local_rows, width)


def solution(mesh):
    n = mesh.shape["row"]
    nx = 4 if n >= 64 else 2
    dims = (n // (2 * nx), nx, 2)
    placed = (P(("groups", "row"), None, None, None), P(), P(("groups", "row"), None))
    return jax.shard_map(
        functools.partial(per_device, dims),
        mesh=mesh,
        in_specs=placed,
        out_specs=P(("groups", "row"), None),
        check_vma=False,
    )
```

```python
import functools
import math

import jax
import jax.numpy as jnp
from jax import lax
from jax.experimental import pallas as pl
from jax.experimental.pallas import tpu as pltpu
from jax.sharding import PartitionSpec as P

GROUP = 8
CHUNKS = 1
LOADS = 4
BLOCK = 32
EARLY = 1
LANES = 128
MESH = pl.DeviceIdType.MESH


def kernel(
    dims, items, rank, total_recent,
    late_hbm, proj_hbm, recent_hbm, out_ref,
    late, proj, recent, turned, fac, other, sketch, mysim, itssim, tf, tb, land,
    load_sem, f_send, f_recv, r_send, r_recv, s_send, s_recv, m_send, m_recv,
):
    nz, nx, nc = dims
    n = nz * nx * nc
    local_recent = recent_hbm.shape[0]
    half = recent.shape[1]
    width = recent_hbm.shape[1]
    pairs, pair_lanes = fac.shape[1:]
    examples = pairs // items
    slab = examples * GROUP
    gw = half // GROUP
    cw = gw // CHUNKS
    bf16, f32 = jnp.bfloat16, jnp.float32
    me = lax.axis_index("row")
    mc = lax.rem(me, nc)
    mx = lax.rem(lax.div(me, nc), nx)
    mz = lax.div(me, nc * nx)
    oc = 1 - mc

    def across(z, d):
        bit = 1
        while bit <= d:
            if d & bit:
                z = z + bit - 2 * bit * lax.rem(lax.div(z, bit), 2)
            bit *= 2
        return z

    peers = []
    for dz in reversed(range(nz)):
        for dx in reversed(range(nx)):
            for dc in (1, 0):
                if dz or dx or dc:
                    z, x = across(mz, dz), lax.rem(mx + dx, nx)
                    c = oc if dc else mc
                    peers.append(((z * nx + x) * nc + c, dc))
    partner = (mz * nx + mx) * nc + oc

    barrier = pltpu.get_barrier_semaphore()
    for index, _ in peers:
        pl.semaphore_signal(barrier, inc=1, device_id={"row": index}, device_id_type=MESH)

    depth = late.shape[2] // LOADS
    load_inputs = []
    for i in range(LOADS):
        part_of = pl.ds(i * depth, depth)
        pair = (
            pltpu.make_async_copy(late_hbm.at[:, :, part_of], late.at[:, :, part_of], load_sem.at[1 + i]),
            pltpu.make_async_copy(proj_hbm.at[part_of], proj.at[part_of], load_sem.at[1 + LOADS + i]),
        )
        for copy in pair:
            copy.start()
        load_inputs.append(pair)

    own_rows = pl.ds(pl.multiple_of(mc * local_recent, local_recent), local_recent)
    its_rows = pl.ds(pl.multiple_of(oc * local_recent, local_recent), local_recent)
    own_half = pl.ds(pl.multiple_of(mc * half, half), half)
    its_half = pl.ds(pl.multiple_of(oc * half, half), half)
    load_recent = pltpu.make_async_copy(
        recent_hbm.at[:, own_half], recent.at[own_rows, :], load_sem.at[0]
    )
    load_recent.start()

    def where(shape, expr):
        r = lax.broadcasted_iota(jnp.int32, shape, 0)
        c = lax.broadcasted_iota(jnp.int32, shape, 1)
        return expr(r, c)

    def onehot(shape, expr):
        return jnp.where(where(shape, expr), 1.0, 0.0).astype(bf16)

    pick = onehot((pairs, 4 * pairs), lambda r, c: r == lax.shift_right_logical(c, 2))
    full = jnp.zeros((4 * pairs, 4 * rank), f32)
    for i, pair in enumerate(load_inputs):
        for copy in pair:
            copy.wait()
        rows = late[:, :, i * depth : (i + 1) * depth].reshape(4 * pairs, depth)
        full = full + jnp.dot(rows, proj[i * depth : (i + 1) * depth, :], preferred_element_type=f32)
    full = jnp.where(
        where(full.shape, lambda r, c: lax.rem(r, 4) == lax.div(c, rank)), full, 0.0
    ).astype(bf16)
    factors = jnp.dot(pick, full, preferred_element_type=f32)
    first, second = factors[:, :pair_lanes], factors[:, pair_lanes:]
    fac[me] = jnp.where(mc == 0, first, second).astype(bf16)
    other[...] = jnp.where(mc == 0, second, first).astype(bf16)

    pl.semaphore_wait(barrier, n - 1)

    sent = []

    def start(src, dst, ss, rs, to):
        copy = pltpu.make_async_remote_copy(
            src_ref=src, dst_ref=dst, send_sem=ss, recv_sem=rs,
            device_id={"row": to}, device_id_type=MESH,
        )
        copy.start()
        sent.append(copy)
        return copy

    for slot, (to, dc) in enumerate(peers):
        start(other if dc else fac.at[me], fac.at[me], f_send.at[slot], f_recv.at[me], to)
    its_recent = start(
        recent_hbm.at[:, its_half], recent.at[own_rows, :], r_send.at[0], r_recv.at[0], partner
    )
    def turn(rows_at, lanes_at):
        for a in range(0, half, 2 * LANES):
            turned[a : a + 2 * LANES, lanes_at] = recent[rows_at, a : a + 2 * LANES].T

    load_recent.wait()
    turn(own_rows, own_rows)
    its_recent.wait_recv()
    turn(its_rows, its_rows)
    rows = GROUP * items
    quad = 4
    many = rank // quad
    tall = many * GROUP
    lift = onehot(
        (rank * GROUP, pair_lanes),
        lambda r, c: c == rank + quad * lax.div(lax.rem(r, tall), GROUP) + lax.div(r, tall),
    )
    twice = onehot((pair_lanes, 2 * rank), lambda r, c: r == lax.rem(c, rank))
    same = where((rank * GROUP, rows), lambda r, c: lax.rem(r, GROUP) == lax.div(c, items))
    left_half = where((tall, 2 * rank), lambda r, c: c < rank)
    unit = GROUP // examples
    units = n // unit
    mine = lax.div(me, unit)

    def arrived(source):
        pltpu.make_async_remote_copy(
            src_ref=other, dst_ref=fac.at[source], send_sem=f_send.at[0], recv_sem=f_recv.at[source],
            device_id={"row": partner}, device_id_type=MESH,
        ).wait_recv()

    def build(u):
        every = fac[pl.ds(u * unit, unit)].reshape(rows, pair_lanes)
        lifted = lax.dot_general(lift, every, (((1,), (1,)), ((), ())), preferred_element_type=f32)
        lifted = jnp.where(same, lifted, 0.0).astype(bf16)
        right = jnp.dot(every, twice, preferred_element_type=f32).astype(bf16)
        outer = jnp.dot(lifted, right, preferred_element_type=f32) * (1.0 / math.sqrt(items))
        low = jnp.where(left_half, outer[:tall], outer[tall : 2 * tall])
        high = jnp.where(left_half, outer[2 * tall : 3 * tall], outer[3 * tall :])
        here = pl.ds(pl.multiple_of(u * GROUP, GROUP), GROUP)
        for a in range(many):
            of = slice(a * GROUP, (a + 1) * GROUP)
            sketch[here, quad * a * rank : (quad * a + 2) * rank] = low[of]
            sketch[here, (quad * a + 2) * rank : (quad * a + 4) * rank] = high[of]

    for j in range(1, unit):
        arrived(mine * unit + lax.rem(me + j, unit))
    build(mine)

    def next_unit(i):
        u = units - i
        u = u - jnp.where(u <= mine, 1, 0)
        for j in range(unit):
            arrived(u * unit + j)
        build(u)

    if units > 8:
        lax.fori_loop(1, units, lambda i, c: (next_unit(i), c)[1], 0)
    else:
        for i in range(1, units):
            next_unit(i)

    blocks = n * examples // BLOCK

    def each_block(body):
        if blocks == 1:
            body(0)
        else:
            lax.fori_loop(0, blocks, lambda b, c: (body(b), c)[1], 0)

    at = lambda b: pl.ds(b * BLOCK, BLOCK)

    def partial(b):
        mysim[at(b)] = jnp.dot(sketch[at(b)].astype(bf16), turned[...], preferred_element_type=f32)

    each_block(partial)
    start(mysim, itssim, s_send.at[0], s_recv.at[0], partner).wait_recv()

    def term(b, k):
        weights = jnp.tanh((mysim[at(b)] + itssim[at(b)]) * (1.0 / math.sqrt(width))).astype(bf16)
        for g in range(GROUP):
            lo = g * gw + k * cw
            got = jnp.dot(weights, recent[:, lo : lo + cw], preferred_element_type=f32)
            for j in range(cw // LANES):
                tf[k, j, pl.ds(b * BLOCK * GROUP + g, BLOCK, stride=GROUP), :] = got[
                    :, j * LANES : (j + 1) * LANES
                ]
        here = pl.ds(b * BLOCK * GROUP, BLOCK * GROUP)
        for j in range(cw // LANES):
            tb.at[k].reshape(n * slab, cw)[here, j * LANES : (j + 1) * LANES] = tf[k, j, here].astype(bf16)

    def remote(src, dst, ss, rs, to):
        return pltpu.make_async_remote_copy(
            src_ref=src, dst_ref=dst, send_sem=ss, recv_sem=rs,
            device_id={"row": to}, device_id_type=MESH,
        )

    places = [(z, x, c) for z in range(nz) for x in range(nx) for c in range(nc)]

    def hand(k, z, x, c, wait=False):
        to = (z * nx + x) * nc + c

        @pl.when(me != to)
        def _():
            copy = remote(
                tb.at[k, z, x, c], land.at[k, me], m_send.at[k, to], m_recv.at[k, me], to
            )
            copy.wait_send() if wait else copy.start()

    def landed(k, source):
        remote(
            tb.at[k, 0, 0, 0], land.at[k, source], m_send.at[k, 0], m_recv.at[k, source], partner
        ).wait_recv()

    early = places[: len(places) * EARLY // nz]
    late_ones = places[len(early) :]
    for k in range(CHUNKS):
        each_block(functools.partial(term, k=k))
        for place in early:
            hand(k, *place)
        land[k, me] = tb[k, mz, mx, mc]
    for place in late_ones:
        for k in range(CHUNKS):
            hand(k, *place)

    for k in range(CHUNKS):
        for source, _ in reversed(peers):
            landed(k, source)
        totals = []
        for c in range(nc):
            total = land[k, c].astype(f32)
            for q in range(1, nz * nx):
                total = total + land[k, q * nc + c].astype(f32)
            totals.append(total)
        rows_out = [
            t[e * GROUP : (e + 1) * GROUP] for e in range(examples) for t in totals
        ]
        out_ref[:, k * cw : (k + 1) * cw] = (
            jnp.concatenate(rows_out, axis=0) * (1.0 / math.sqrt(total_recent))
        ).astype(bf16)

    for k in range(CHUNKS):
        for place in places:
            hand(k, *place, wait=True)
    for copy in sent:
        copy.wait_send()


def per_device(dims, late_grads, projections, recent_sketches):
    nz, nx, nc = dims
    local_rows, items, kinds, width_in = late_grads.shape
    rank = projections.shape[1] // 4
    local_recent, width = recent_sketches.shape
    n = nz * nx * nc
    half = width // 2
    slab, cw = local_rows * GROUP, half // GROUP // CHUNKS
    every = n * local_rows
    bf16, f32 = jnp.bfloat16, jnp.float32
    dma = pltpu.SemaphoreType.DMA
    out = pl.pallas_call(
        functools.partial(kernel, dims, items, rank, local_recent * n),
        out_shape=pltpu.VMEM((2 * slab, half // GROUP), bf16),
        in_specs=[pl.BlockSpec(memory_space=pl.ANY)] * 3,
        out_specs=pl.BlockSpec(memory_space=pltpu.VMEM),
        scratch_shapes=[
            pltpu.VMEM((local_rows * items, kinds, width_in), bf16),
            pltpu.VMEM(projections.shape, bf16),
            pltpu.VMEM((nc * local_recent, half), bf16),
            pltpu.VMEM((half, nc * local_recent), bf16),
            pltpu.VMEM((n, local_rows * items, 2 * rank), bf16),
            pltpu.VMEM((local_rows * items, 2 * rank), bf16),
            pltpu.VMEM((every, half), f32),
            pltpu.VMEM((every, nc * local_recent), f32),
            pltpu.VMEM((every, nc * local_recent), f32),
            pltpu.VMEM((CHUNKS, cw // LANES, every * GROUP, LANES), f32),
            pltpu.VMEM((CHUNKS, nz, nx, nc, slab, cw), bf16),
            pltpu.VMEM((CHUNKS, n, slab, cw), bf16),
            dma((1 + 2 * LOADS,)),
            dma((n - 1,)),
            dma((n,)),
            dma((1,)),
            dma((1,)),
            dma((1,)),
            dma((1,)),
            dma((CHUNKS, n)),
            dma((CHUNKS, n)),
        ],
        compiler_params=pltpu.CompilerParams(
            collective_id=0, has_side_effects=True, vmem_limit_bytes=60 * 1024 * 1024
        ),
    )(late_grads.reshape(local_rows * items, kinds, width_in), projections, recent_sketches)
    return out.reshape(local_rows, width)


def solution(mesh):
    n = mesh.shape["row"]
    nx = 4 if n >= 64 else 2
    dims = (n // (2 * nx), nx, 2)
    placed = (P(("groups", "row"), None, None, None), P(), P(("groups", "row"), None))
    return jax.shard_map(
        functools.partial(per_device, dims),
        mesh=mesh,
        in_specs=placed,
        out_specs=P(("groups", "row"), None),
        check_vma=False,
    )
```

```python
import functools
import math

import jax
import jax.numpy as jnp
from jax import lax
from jax.experimental import pallas as pl
from jax.experimental.pallas import tpu as pltpu
from jax.sharding import PartitionSpec as P

GROUP = 8
CHUNKS = 1
LOADS = 4
BLOCK = 32
EARLY = 1
LANES = 128
MESH = pl.DeviceIdType.MESH


def kernel(
    dims, items, rank, total_recent,
    late_hbm, proj_hbm, recent_hbm, out_ref,
    late, proj, recent, turned, fac, other, mysim, itssim, tf, tb, land,
    load_sem, f_send, f_recv, r_send, r_recv, s_send, s_recv, m_send, m_recv,
):
    nz, nx, nc = dims
    n = nz * nx * nc
    local_recent = recent_hbm.shape[0]
    half = recent.shape[1]
    width = recent_hbm.shape[1]
    pairs, pair_lanes = fac.shape[1:]
    examples = pairs // items
    slab = examples * GROUP
    gw = half // GROUP
    cw = gw // CHUNKS
    bf16, f32 = jnp.bfloat16, jnp.float32
    me = lax.axis_index("row")
    mc = lax.rem(me, nc)
    mx = lax.rem(lax.div(me, nc), nx)
    mz = lax.div(me, nc * nx)
    oc = 1 - mc

    def across(z, d):
        bit = 1
        while bit <= d:
            if d & bit:
                z = z + bit - 2 * bit * lax.rem(lax.div(z, bit), 2)
            bit *= 2
        return z

    peers = []
    for dz in reversed(range(nz)):
        for dx in reversed(range(nx)):
            for dc in (1, 0):
                if dz or dx or dc:
                    z, x = across(mz, dz), lax.rem(mx + dx, nx)
                    c = oc if dc else mc
                    peers.append(((z * nx + x) * nc + c, dc))
    partner = (mz * nx + mx) * nc + oc

    barrier = pltpu.get_barrier_semaphore()
    for index, _ in peers:
        pl.semaphore_signal(barrier, inc=1, device_id={"row": index}, device_id_type=MESH)

    depth = late.shape[2] // LOADS
    load_inputs = []
    for i in range(LOADS):
        part_of = pl.ds(i * depth, depth)
        pair = (
            pltpu.make_async_copy(late_hbm.at[:, :, part_of], late.at[:, :, part_of], load_sem.at[1 + i]),
            pltpu.make_async_copy(proj_hbm.at[part_of], proj.at[part_of], load_sem.at[1 + LOADS + i]),
        )
        for copy in pair:
            copy.start()
        load_inputs.append(pair)

    own_rows = pl.ds(pl.multiple_of(mc * local_recent, local_recent), local_recent)
    its_rows = pl.ds(pl.multiple_of(oc * local_recent, local_recent), local_recent)
    own_half = pl.ds(pl.multiple_of(mc * half, half), half)
    its_half = pl.ds(pl.multiple_of(oc * half, half), half)
    load_recent = pltpu.make_async_copy(
        recent_hbm.at[:, own_half], recent.at[own_rows, :], load_sem.at[0]
    )
    load_recent.start()

    def where(shape, expr):
        r = lax.broadcasted_iota(jnp.int32, shape, 0)
        c = lax.broadcasted_iota(jnp.int32, shape, 1)
        return expr(r, c)

    def onehot(shape, expr):
        return jnp.where(where(shape, expr), 1.0, 0.0).astype(bf16)

    pick = onehot((pairs, 4 * pairs), lambda r, c: r == lax.shift_right_logical(c, 2))
    full = jnp.zeros((4 * pairs, 4 * rank), f32)
    for i, pair in enumerate(load_inputs):
        for copy in pair:
            copy.wait()
        rows = late[:, :, i * depth : (i + 1) * depth].reshape(4 * pairs, depth)
        full = full + jnp.dot(rows, proj[i * depth : (i + 1) * depth, :], preferred_element_type=f32)
    full = jnp.where(
        where(full.shape, lambda r, c: lax.rem(r, 4) == lax.div(c, rank)), full, 0.0
    ).astype(bf16)
    factors = jnp.dot(pick, full, preferred_element_type=f32)
    first, second = factors[:, :pair_lanes], factors[:, pair_lanes:]
    fac[me] = jnp.where(mc == 0, first, second).astype(bf16)
    other[...] = jnp.where(mc == 0, second, first).astype(bf16)

    pl.semaphore_wait(barrier, n - 1)

    sent = []

    def start(src, dst, ss, rs, to):
        copy = pltpu.make_async_remote_copy(
            src_ref=src, dst_ref=dst, send_sem=ss, recv_sem=rs,
            device_id={"row": to}, device_id_type=MESH,
        )
        copy.start()
        sent.append(copy)
        return copy

    for slot, (to, dc) in enumerate(peers):
        start(other if dc else fac.at[me], fac.at[me], f_send.at[slot], f_recv.at[me], to)
    its_recent = start(
        recent_hbm.at[:, its_half], recent.at[own_rows, :], r_send.at[0], r_recv.at[0], partner
    )
    def turn(rows_at, lanes_at):
        for a in range(0, half, 2 * LANES):
            turned[a : a + 2 * LANES, lanes_at] = recent[rows_at, a : a + 2 * LANES].T

    load_recent.wait()
    turn(own_rows, own_rows)
    its_recent.wait_recv()
    turn(its_rows, its_rows)
    rows = BLOCK * items
    lanes = GROUP * items
    quad = 4
    many = rank // quad
    tall = many * GROUP
    units = BLOCK // GROUP
    blocks = n * examples // BLOCK
    lift = onehot(
        (rank * GROUP, pair_lanes),
        lambda r, c: c == rank + quad * lax.div(lax.rem(r, tall), GROUP) + lax.div(r, tall),
    )
    twice = onehot((pair_lanes, 2 * rank), lambda r, c: r == lax.rem(c, rank))
    same = onehot((tall, lanes), lambda r, c: lax.rem(r, GROUP) == lax.div(c, items))
    left_lanes = where((rows, 2 * rank), lambda r, c: c < rank)

    for source, _ in peers:
        pltpu.make_async_remote_copy(
            src_ref=other, dst_ref=fac.at[source], send_sem=f_send.at[0], recv_sem=f_recv.at[source],
            device_id={"row": partner}, device_id_type=MESH,
        ).wait_recv()

    def build(b):
        every = fac[pl.ds(b * (BLOCK // examples), BLOCK // examples)].reshape(rows, pair_lanes)
        lifted = lax.dot_general(
            lift, every, (((1,), (1,)), ((), ())), preferred_element_type=f32
        ).astype(bf16)
        right = jnp.dot(every, twice, preferred_element_type=f32)
        first = jnp.where(left_lanes, right, 0.0).astype(bf16)
        second = jnp.where(left_lanes, 0.0, right).astype(bf16)
        outer = []
        for u in range(units):
            of = slice(u * lanes, (u + 1) * lanes)
            four = [lifted[i * tall : (i + 1) * tall, of] * same for i in range(quad)]
            outer.append(
                jnp.dot(
                    jnp.concatenate(
                        [jnp.concatenate(four[:2], axis=1), jnp.concatenate(four[2:], axis=1)], axis=0
                    ),
                    jnp.concatenate([first[of], second[of]], axis=0),
                    preferred_element_type=f32,
                )
            )
        pieces = []
        for a in range(many):
            for side in range(2):
                at = side * tall + a * GROUP
                pieces.append(jnp.concatenate([o[at : at + GROUP] for o in outer], axis=0))
        return (jnp.concatenate(pieces, axis=1) * (1.0 / math.sqrt(items))).astype(bf16)

    def each_block(body):
        if blocks == 1:
            body(0)
        else:
            lax.fori_loop(0, blocks, lambda b, c: (body(b), c)[1], 0)

    at = lambda b: pl.ds(b * BLOCK, BLOCK)

    def partial(b):
        mysim[at(b)] = jnp.dot(build(b), turned[...], preferred_element_type=f32)

    each_block(partial)
    start(mysim, itssim, s_send.at[0], s_recv.at[0], partner).wait_recv()

    def term(b, k):
        weights = jnp.tanh((mysim[at(b)] + itssim[at(b)]) * (1.0 / math.sqrt(width))).astype(bf16)
        for g in range(GROUP):
            lo = g * gw + k * cw
            got = jnp.dot(weights, recent[:, lo : lo + cw], preferred_element_type=f32)
            for j in range(cw // LANES):
                tf[k, j, pl.ds(b * BLOCK * GROUP + g, BLOCK, stride=GROUP), :] = got[
                    :, j * LANES : (j + 1) * LANES
                ]
        here = pl.ds(b * BLOCK * GROUP, BLOCK * GROUP)
        for j in range(cw // LANES):
            tb.at[k].reshape(n * slab, cw)[here, j * LANES : (j + 1) * LANES] = tf[k, j, here].astype(bf16)

    def remote(src, dst, ss, rs, to):
        return pltpu.make_async_remote_copy(
            src_ref=src, dst_ref=dst, send_sem=ss, recv_sem=rs,
            device_id={"row": to}, device_id_type=MESH,
        )

    places = [(z, x, c) for z in range(nz) for x in range(nx) for c in range(nc)]

    def hand(k, z, x, c, wait=False):
        to = (z * nx + x) * nc + c

        @pl.when(me != to)
        def _():
            copy = remote(
                tb.at[k, z, x, c], land.at[k, me], m_send.at[k, to], m_recv.at[k, me], to
            )
            copy.wait_send() if wait else copy.start()

    def landed(k, source):
        remote(
            tb.at[k, 0, 0, 0], land.at[k, source], m_send.at[k, 0], m_recv.at[k, source], partner
        ).wait_recv()

    early = places[: len(places) * EARLY // nz]
    late_ones = places[len(early) :]
    for k in range(CHUNKS):
        each_block(functools.partial(term, k=k))
        for place in early:
            hand(k, *place)
        land[k, me] = tb[k, mz, mx, mc]
    for place in late_ones:
        for k in range(CHUNKS):
            hand(k, *place)

    for k in range(CHUNKS):
        for source, _ in reversed(peers):
            landed(k, source)
        totals = []
        for c in range(nc):
            total = land[k, c].astype(f32)
            for q in range(1, nz * nx):
                total = total + land[k, q * nc + c].astype(f32)
            totals.append(total)
        rows_out = [
            t[e * GROUP : (e + 1) * GROUP] for e in range(examples) for t in totals
        ]
        out_ref[:, k * cw : (k + 1) * cw] = (
            jnp.concatenate(rows_out, axis=0) * (1.0 / math.sqrt(total_recent))
        ).astype(bf16)

    for k in range(CHUNKS):
        for place in places:
            hand(k, *place, wait=True)
    for copy in sent:
        copy.wait_send()


def per_device(dims, late_grads, projections, recent_sketches):
    nz, nx, nc = dims
    local_rows, items, kinds, width_in = late_grads.shape
    rank = projections.shape[1] // 4
    local_recent, width = recent_sketches.shape
    n = nz * nx * nc
    half = width // 2
    slab, cw = local_rows * GROUP, half // GROUP // CHUNKS
    every = n * local_rows
    bf16, f32 = jnp.bfloat16, jnp.float32
    dma = pltpu.SemaphoreType.DMA
    out = pl.pallas_call(
        functools.partial(kernel, dims, items, rank, local_recent * n),
        out_shape=pltpu.VMEM((2 * slab, half // GROUP), bf16),
        in_specs=[pl.BlockSpec(memory_space=pl.ANY)] * 3,
        out_specs=pl.BlockSpec(memory_space=pltpu.VMEM),
        scratch_shapes=[
            pltpu.VMEM((local_rows * items, kinds, width_in), bf16),
            pltpu.VMEM(projections.shape, bf16),
            pltpu.VMEM((nc * local_recent, half), bf16),
            pltpu.VMEM((half, nc * local_recent), bf16),
            pltpu.VMEM((n, local_rows * items, 2 * rank), bf16),
            pltpu.VMEM((local_rows * items, 2 * rank), bf16),
            pltpu.VMEM((every, nc * local_recent), f32),
            pltpu.VMEM((every, nc * local_recent), f32),
            pltpu.VMEM((CHUNKS, cw // LANES, every * GROUP, LANES), f32),
            pltpu.VMEM((CHUNKS, nz, nx, nc, slab, cw), bf16),
            pltpu.VMEM((CHUNKS, n, slab, cw), bf16),
            dma((1 + 2 * LOADS,)),
            dma((n - 1,)),
            dma((n,)),
            dma((1,)),
            dma((1,)),
            dma((1,)),
            dma((1,)),
            dma((CHUNKS, n)),
            dma((CHUNKS, n)),
        ],
        compiler_params=pltpu.CompilerParams(
            collective_id=0, has_side_effects=True, vmem_limit_bytes=60 * 1024 * 1024
        ),
    )(late_grads.reshape(local_rows * items, kinds, width_in), projections, recent_sketches)
    return out.reshape(local_rows, width)


def solution(mesh):
    n = mesh.shape["row"]
    nx = 4 if n >= 64 else 2
    dims = (n // (2 * nx), nx, 2)
    placed = (P(("groups", "row"), None, None, None), P(), P(("groups", "row"), None))
    return jax.shard_map(
        functools.partial(per_device, dims),
        mesh=mesh,
        in_specs=placed,
        out_specs=P(("groups", "row"), None),
        check_vma=False,
    )
```

```python
import functools
import math

import jax
import jax.numpy as jnp
from jax import lax
from jax.experimental import pallas as pl
from jax.experimental.pallas import tpu as pltpu
from jax.sharding import PartitionSpec as P

GROUP = 8
CHUNKS = 1
LOADS = 4
BLOCK = 16
HALVES = 2
PIECES = 2
DIRECT = 1
FOLDING = 1
LANES = 128
MESH = pl.DeviceIdType.MESH


def kernel(
    dims, items, rank, total_recent,
    late_hbm, proj_hbm, recent_hbm, out_ref,
    late, proj, recent, turned, fac, other, mysim, itssim, tf, tb, xland, xb, land,
    load_sem, f_send, f_recv, r_send, r_recv, s_send, s_recv, x_send, x_recv, m_send, m_recv,
):
    nz, nx, nc = dims
    n = nz * nx * nc
    local_recent = recent_hbm.shape[0]
    half = recent.shape[1]
    width = recent_hbm.shape[1]
    pairs, pair_lanes = fac.shape[1:]
    examples = pairs // items
    slab = examples * GROUP
    gw = half // GROUP
    cw = gw // CHUNKS
    bf16, f32 = jnp.bfloat16, jnp.float32
    me = lax.axis_index("row")
    mc = lax.rem(me, nc)
    mx = lax.rem(lax.div(me, nc), nx)
    mz = lax.div(me, nc * nx)
    oc = 1 - mc

    def across(z, d):
        bit = 1
        while bit <= d:
            if d & bit:
                z = z + bit - 2 * bit * lax.rem(lax.div(z, bit), 2)
            bit *= 2
        return z

    peers = []
    for dz in reversed(range(nz)):
        for dx in reversed(range(nx)):
            for dc in (1, 0):
                if dz or dx or dc:
                    z, x = across(mz, dz), lax.rem(mx + dx, nx)
                    c = oc if dc else mc
                    peers.append(((z * nx + x) * nc + c, dc))
    partner = (mz * nx + mx) * nc + oc

    barrier = pltpu.get_barrier_semaphore()
    for index, _ in peers:
        pl.semaphore_signal(barrier, inc=1, device_id={"row": index}, device_id_type=MESH)

    depth = late.shape[2] // LOADS
    load_inputs = []
    for i in range(LOADS):
        part_of = pl.ds(i * depth, depth)
        pair = (
            pltpu.make_async_copy(late_hbm.at[:, :, part_of], late.at[:, :, part_of], load_sem.at[1 + i]),
            pltpu.make_async_copy(proj_hbm.at[part_of], proj.at[part_of], load_sem.at[1 + LOADS + i]),
        )
        for copy in pair:
            copy.start()
        load_inputs.append(pair)

    own_rows = pl.ds(pl.multiple_of(mc * local_recent, local_recent), local_recent)
    its_rows = pl.ds(pl.multiple_of(oc * local_recent, local_recent), local_recent)
    own_half = pl.ds(pl.multiple_of(mc * half, half), half)
    load_recent = pltpu.make_async_copy(
        recent_hbm.at[:, own_half], recent.at[own_rows, :], load_sem.at[0]
    )
    load_recent.start()

    def where(shape, expr):
        r = lax.broadcasted_iota(jnp.int32, shape, 0)
        c = lax.broadcasted_iota(jnp.int32, shape, 1)
        return expr(r, c)

    def onehot(shape, expr):
        return jnp.where(where(shape, expr), 1.0, 0.0).astype(bf16)

    pick = onehot((pairs, 4 * pairs), lambda r, c: r == lax.shift_right_logical(c, 2))
    full = jnp.zeros((4 * pairs, 4 * rank), f32)
    for i, pair in enumerate(load_inputs):
        for copy in pair:
            copy.wait()
        rows = late[:, :, i * depth : (i + 1) * depth].reshape(4 * pairs, depth)
        full = full + jnp.dot(rows, proj[i * depth : (i + 1) * depth, :], preferred_element_type=f32)
    full = jnp.where(
        where(full.shape, lambda r, c: lax.rem(r, 4) == lax.div(c, rank)), full, 0.0
    ).astype(bf16)
    factors = jnp.dot(pick, full, preferred_element_type=f32)
    first, second = factors[:, :pair_lanes], factors[:, pair_lanes:]
    fac[me] = jnp.where(mc == 0, first, second).astype(bf16)
    other[...] = jnp.where(mc == 0, second, first).astype(bf16)

    pl.semaphore_wait(barrier, n - 1)

    sent = []

    def start(src, dst, ss, rs, to):
        copy = pltpu.make_async_remote_copy(
            src_ref=src, dst_ref=dst, send_sem=ss, recv_sem=rs,
            device_id={"row": to}, device_id_type=MESH,
        )
        copy.start()
        sent.append(copy)
        return copy

    for slot, (to, dc) in enumerate(peers):
        start(other if dc else fac.at[me], fac.at[me], f_send.at[slot], f_recv.at[me], to)
    piece = half // PIECES
    its_recent = [
        start(
            recent_hbm.at[:, pl.ds(pl.multiple_of(oc * half + p * piece, piece), piece)],
            recent.at[own_rows, p * piece : (p + 1) * piece], r_send.at[p], r_recv.at[p], partner,
        )
        for p in range(PIECES)
    ]

    def turn(rows_at, lanes_at, p):
        for a in range(p * piece, (p + 1) * piece, 2 * LANES):
            turned[a : a + 2 * LANES, lanes_at] = recent[rows_at, a : a + 2 * LANES].T

    folded = lax.rem(mz, nz // 2) >= DIRECT

    @pl.when(folded)
    def _():
        for z in range(nz // 2):
            for d in range(1, nx):
                for c in range(FOLDING, nc):
                    away = (1 - lax.div(mz, nz // 2)) * (nz // 2) + z
                    source = (away * nx + lax.rem(mx + d, nx)) * nc + c
                    for k in range(CHUNKS):
                        land[k, source] = jnp.zeros((slab, cw), bf16)

    load_recent.wait()
    for p in range(PIECES):
        turn(own_rows, own_rows, p)
    for p in range(PIECES):
        its_recent[p].wait_recv()
        turn(its_rows, its_rows, p)
    rows = BLOCK * items
    lanes = GROUP * items
    quad = 4
    many = rank // quad
    tall = many * GROUP
    units = BLOCK // GROUP
    blocks = n * examples // BLOCK // HALVES
    lift = onehot(
        (rank * GROUP, pair_lanes),
        lambda r, c: c == rank + quad * lax.div(lax.rem(r, tall), GROUP) + lax.div(r, tall),
    )
    twice = onehot((pair_lanes, 2 * rank), lambda r, c: r == lax.rem(c, rank))
    same = onehot((tall, lanes), lambda r, c: lax.rem(r, GROUP) == lax.div(c, items))
    left_lanes = where((rows, 2 * rank), lambda r, c: c < rank)

    def arrived(source):
        @pl.when(me != source)
        def _():
            pltpu.make_async_remote_copy(
                src_ref=other, dst_ref=fac.at[source], send_sem=f_send.at[0],
                recv_sem=f_recv.at[source], device_id={"row": partner}, device_id_type=MESH,
            ).wait_recv()

    def build(b):
        every = fac[pl.ds(b * (BLOCK // examples), BLOCK // examples)].reshape(rows, pair_lanes)
        lifted = lax.dot_general(
            lift, every, (((1,), (1,)), ((), ())), preferred_element_type=f32
        ).astype(bf16)
        right = jnp.dot(every, twice, preferred_element_type=f32)
        first = jnp.where(left_lanes, right, 0.0).astype(bf16)
        second = jnp.where(left_lanes, 0.0, right).astype(bf16)
        outer = []
        for u in range(units):
            of = slice(u * lanes, (u + 1) * lanes)
            four = [lifted[i * tall : (i + 1) * tall, of] * same for i in range(quad)]
            outer.append(
                jnp.dot(
                    jnp.concatenate(
                        [jnp.concatenate(four[:2], axis=1), jnp.concatenate(four[2:], axis=1)], axis=0
                    ),
                    jnp.concatenate([first[of], second[of]], axis=0),
                    preferred_element_type=f32,
                )
            )
        pieces = []
        for a in range(many):
            for side in range(2):
                at = side * tall + a * GROUP
                pieces.append(jnp.concatenate([o[at : at + GROUP] for o in outer], axis=0))
        return (jnp.concatenate(pieces, axis=1) * (1.0 / math.sqrt(items))).astype(bf16)

    def each_block(half_at, body):
        if blocks == 1:
            body(half_at)
        else:
            lax.fori_loop(half_at * blocks, (half_at + 1) * blocks, lambda b, c: (body(b), c)[1], 0)

    at = lambda b: pl.ds(b * BLOCK, BLOCK)

    def partial(b):
        mysim[at(b)] = jnp.dot(build(b), turned[...], preferred_element_type=f32)

    swaps = []
    for h in range(HALVES):
        for source in range(h * n // HALVES, (h + 1) * n // HALVES):
            arrived(source)
        each_block(h, partial)
        of = pl.ds(h * blocks * BLOCK, blocks * BLOCK)
        swaps.append(start(mysim.at[of], itssim.at[of], s_send.at[h], s_recv.at[h], partner))

    def term(b, k):
        weights = jnp.tanh((mysim[at(b)] + itssim[at(b)]) * (1.0 / math.sqrt(width))).astype(bf16)
        for g in range(GROUP):
            lo = g * gw + k * cw
            got = jnp.dot(weights, recent[:, lo : lo + cw], preferred_element_type=f32)
            for j in range(cw // LANES):
                tf[k, j, pl.ds(b * BLOCK * GROUP + g, BLOCK, stride=GROUP), :] = got[
                    :, j * LANES : (j + 1) * LANES
                ]
        here = pl.ds(b * BLOCK * GROUP, BLOCK * GROUP)
        for j in range(cw // LANES):
            tb.at[k].reshape(n * slab, cw)[here, j * LANES : (j + 1) * LANES] = tf[k, j, here].astype(bf16)

    def remote(src, dst, ss, rs, to):
        return pltpu.make_async_remote_copy(
            src_ref=src, dst_ref=dst, send_sem=ss, recv_sem=rs,
            device_id={"row": to}, device_id_type=MESH,
        )

    places = [(z, x, c) for z in range(nz) for x in range(nx) for c in range(nc)]

    hz = nz // 2
    others = hz - DIRECT
    upper = lax.div(mz, hz)
    first = (1 - upper) * hz + DIRECT
    folds = mc >= FOLDING

    def crosses(z):
        return upper != z // hz

    def hand(k, z, x, c, wait=False):
        to = (z * nx + x) * nc + c
        leaves = me != to
        if z % hz >= DIRECT:
            leaves = leaves & jnp.logical_not(crosses(z) & folds)

        @pl.when(leaves)
        def _():
            copy = remote(
                tb.at[k, z, x, c], land.at[k, me], m_send.at[k, to], m_recv.at[k, me], to
            )
            copy.wait_send() if wait else copy.start()

    def sideways(k, d):
        x = lax.rem(mx + d, nx)
        return remote(
            tb.at[k, pl.ds(first, others), x], xland.at[k, d - 1], x_send.at[k, d - 1],
            x_recv.at[k, d - 1], (mz * nx + x) * nc + mc,
        )

    def onward(k, d, c):
        to = ((first + d) * nx + mx) * nc + c
        return remote(xb.at[k, d, c], land.at[k, me], m_send.at[k, to], m_recv.at[k, me], to)

    def landed(k, source):
        remote(
            tb.at[k, 0, 0, 0], land.at[k, source], m_send.at[k, 0], m_recv.at[k, source], partner
        ).wait_recv()

    def aside(k, h):
        @pl.when(folds & (upper != h))
        def _():
            for d in range(1, nx):
                sideways(k, d).start()

    for h in range(HALVES):
        swaps[h].wait_recv()
        for k in range(CHUNKS):
            each_block(h, functools.partial(term, k=k))
            aside(k, h)
            for place in places[h * n // HALVES : (h + 1) * n // HALVES]:
                hand(k, *place)

            @pl.when(lax.div(mz, hz) == h)
            def _():
                land[k, me] = tb[k, mz, mx, mc]

    @pl.when(folds)
    def _():
        for k in range(CHUNKS):
            total = tb[k, pl.ds(first, others), mx].astype(f32)
            for d in range(1, nx):
                sideways(k, d).wait_recv()
                total = total + xland[k, d - 1].astype(f32)
            xb[k] = total.astype(bf16)
            for d in range(others):
                for c in range(nc):
                    onward(k, d, c).start()

    for copy in sent:
        copy.wait_send()
    for k in range(CHUNKS):
        for place in places[: n // HALVES]:
            hand(k, *place, wait=True)

    for k in range(CHUNKS):
        for z, x, c in reversed(places):
            source = (z * nx + x) * nc + c
            comes = me != source
            if c >= FOLDING:
                comes = comes & jnp.logical_not(crosses(z) & folded & (mx != x))

            @pl.when(comes)
            def _():
                landed(k, source)
        totals = []
        for c in range(nc):
            total = land[k, c].astype(f32)
            for q in range(1, nz * nx):
                total = total + land[k, q * nc + c].astype(f32)
            totals.append(total)
        rows_out = [
            t[e * GROUP : (e + 1) * GROUP] for e in range(examples) for t in totals
        ]
        out_ref[:, k * cw : (k + 1) * cw] = (
            jnp.concatenate(rows_out, axis=0) * (1.0 / math.sqrt(total_recent))
        ).astype(bf16)

    for k in range(CHUNKS):
        for place in places[n // HALVES :]:
            hand(k, *place, wait=True)

    @pl.when(folds)
    def _():
        for k in range(CHUNKS):
            for d in range(1, nx):
                sideways(k, d).wait_send()
            for d in range(others):
                for c in range(nc):
                    onward(k, d, c).wait_send()


def per_device(dims, late_grads, projections, recent_sketches):
    nz, nx, nc = dims
    local_rows, items, kinds, width_in = late_grads.shape
    rank = projections.shape[1] // 4
    local_recent, width = recent_sketches.shape
    n = nz * nx * nc
    half = width // 2
    slab, cw = local_rows * GROUP, half // GROUP // CHUNKS
    every = n * local_rows
    bf16, f32 = jnp.bfloat16, jnp.float32
    dma = pltpu.SemaphoreType.DMA
    out = pl.pallas_call(
        functools.partial(kernel, dims, items, rank, local_recent * n),
        out_shape=pltpu.VMEM((2 * slab, half // GROUP), bf16),
        in_specs=[pl.BlockSpec(memory_space=pl.ANY)] * 3,
        out_specs=pl.BlockSpec(memory_space=pltpu.VMEM),
        scratch_shapes=[
            pltpu.VMEM((local_rows * items, kinds, width_in), bf16),
            pltpu.VMEM(projections.shape, bf16),
            pltpu.VMEM((nc * local_recent, half), bf16),
            pltpu.VMEM((half, nc * local_recent), bf16),
            pltpu.VMEM((n, local_rows * items, 2 * rank), bf16),
            pltpu.VMEM((local_rows * items, 2 * rank), bf16),
            pltpu.VMEM((every, nc * local_recent), f32),
            pltpu.VMEM((every, nc * local_recent), f32),
            pltpu.VMEM((CHUNKS, cw // LANES, every * GROUP, LANES), f32),
            pltpu.VMEM((CHUNKS, nz, nx, nc, slab, cw), bf16),
            pltpu.VMEM((CHUNKS, nx - 1, nz // 2 - DIRECT, nc, slab, cw), bf16),
            pltpu.VMEM((CHUNKS, nz // 2 - DIRECT, nc, slab, cw), bf16),
            pltpu.VMEM((CHUNKS, n, slab, cw), bf16),
            dma((1 + 2 * LOADS,)),
            dma((n - 1,)),
            dma((n,)),
            dma((PIECES,)),
            dma((PIECES,)),
            dma((HALVES,)),
            dma((HALVES,)),
            dma((CHUNKS, nx - 1)),
            dma((CHUNKS, nx - 1)),
            dma((CHUNKS, n)),
            dma((CHUNKS, n)),
        ],
        compiler_params=pltpu.CompilerParams(
            collective_id=0, has_side_effects=True, vmem_limit_bytes=60 * 1024 * 1024
        ),
    )(late_grads.reshape(local_rows * items, kinds, width_in), projections, recent_sketches)
    return out.reshape(local_rows, width)


def solution(mesh):
    n = mesh.shape["row"]
    nx = 4 if n >= 64 else 2
    dims = (n // (2 * nx), nx, 2)
    placed = (P(("groups", "row"), None, None, None), P(), P(("groups", "row"), None))
    return jax.shard_map(
        functools.partial(per_device, dims),
        mesh=mesh,
        in_specs=placed,
        out_specs=P(("groups", "row"), None),
        check_vma=False,
    )
```

```python
import functools
import math

import jax
import jax.numpy as jnp
from jax import lax
from jax.experimental import pallas as pl
from jax.experimental.pallas import tpu as pltpu
from jax.sharding import PartitionSpec as P

GROUP = 8
CHUNKS = 1
LOADS = 4
BLOCK = 16
HALVES = 2
FIRSTW = 0
PIECES = 2
DIRECT = 1
FOLDING = 1
LANES = 128
MESH = pl.DeviceIdType.MESH


def kernel(
    dims, items, rank, total_recent,
    late_hbm, proj_hbm, recent_hbm, out_ref,
    late, proj, recent, turned, fac, other, mysim, itssim, tf, tb, xland, xb, land,
    load_sem, f_send, f_recv, r_send, r_recv, s_send, s_recv, x_send, x_recv, m_send, m_recv,
):
    nz, nx, nc = dims
    n = nz * nx * nc
    local_recent = recent_hbm.shape[0]
    half = recent.shape[1]
    width = recent_hbm.shape[1]
    pairs, pair_lanes = fac.shape[1:]
    examples = pairs // items
    slab = examples * GROUP
    gw = half // GROUP
    cw = gw // CHUNKS
    bf16, f32 = jnp.bfloat16, jnp.float32
    me = lax.axis_index("row")
    mc = lax.rem(me, nc)
    mx = lax.rem(lax.div(me, nc), nx)
    mz = lax.div(me, nc * nx)
    oc = 1 - mc

    def across(z, d):
        bit = 1
        while bit <= d:
            if d & bit:
                z = z + bit - 2 * bit * lax.rem(lax.div(z, bit), 2)
            bit *= 2
        return z

    peers = []
    for dz in reversed(range(nz)):
        for dx in reversed(range(nx)):
            for dc in (1, 0):
                if dz or dx or dc:
                    z, x = across(mz, dz), lax.rem(mx + dx, nx)
                    c = oc if dc else mc
                    peers.append(((z * nx + x) * nc + c, dc))
    partner = (mz * nx + mx) * nc + oc

    barrier = pltpu.get_barrier_semaphore()
    for index, _ in peers:
        pl.semaphore_signal(barrier, inc=1, device_id={"row": index}, device_id_type=MESH)

    depth = late.shape[2] // LOADS
    load_inputs = []
    for i in range(LOADS):
        part_of = pl.ds(i * depth, depth)
        pair = (
            pltpu.make_async_copy(late_hbm.at[:, :, part_of], late.at[:, :, part_of], load_sem.at[1 + i]),
            pltpu.make_async_copy(proj_hbm.at[part_of], proj.at[part_of], load_sem.at[1 + LOADS + i]),
        )
        for copy in pair:
            copy.start()
        load_inputs.append(pair)

    own_rows = pl.ds(pl.multiple_of(mc * local_recent, local_recent), local_recent)
    its_rows = pl.ds(pl.multiple_of(oc * local_recent, local_recent), local_recent)
    own_half = pl.ds(pl.multiple_of(mc * half, half), half)
    load_recent = pltpu.make_async_copy(
        recent_hbm.at[:, own_half], recent.at[own_rows, :], load_sem.at[0]
    )
    load_recent.start()

    def where(shape, expr):
        r = lax.broadcasted_iota(jnp.int32, shape, 0)
        c = lax.broadcasted_iota(jnp.int32, shape, 1)
        return expr(r, c)

    def onehot(shape, expr):
        return jnp.where(where(shape, expr), 1.0, 0.0).astype(bf16)

    pick = onehot((pairs, 4 * pairs), lambda r, c: r == lax.shift_right_logical(c, 2))
    full = jnp.zeros((4 * pairs, 4 * rank), f32)
    for i, pair in enumerate(load_inputs):
        for copy in pair:
            copy.wait()
        rows = late[:, :, i * depth : (i + 1) * depth].reshape(4 * pairs, depth)
        full = full + jnp.dot(rows, proj[i * depth : (i + 1) * depth, :], preferred_element_type=f32)
    full = jnp.where(
        where(full.shape, lambda r, c: lax.rem(r, 4) == lax.div(c, rank)), full, 0.0
    ).astype(bf16)
    factors = jnp.dot(pick, full, preferred_element_type=f32)
    first, second = factors[:, :pair_lanes], factors[:, pair_lanes:]
    fac[me] = jnp.where(mc == 0, first, second).astype(bf16)
    other[...] = jnp.where(mc == 0, second, first).astype(bf16)

    pl.semaphore_wait(barrier, n - 1)

    sent = []

    def start(src, dst, ss, rs, to):
        copy = pltpu.make_async_remote_copy(
            src_ref=src, dst_ref=dst, send_sem=ss, recv_sem=rs,
            device_id={"row": to}, device_id_type=MESH,
        )
        copy.start()
        sent.append(copy)
        return copy

    for slot, (to, dc) in enumerate(peers):
        start(other if dc else fac.at[me], fac.at[me], f_send.at[slot], f_recv.at[me], to)
    piece = half // PIECES
    its_recent = [
        start(
            recent_hbm.at[:, pl.ds(pl.multiple_of(oc * half + p * piece, piece), piece)],
            recent.at[own_rows, p * piece : (p + 1) * piece], r_send.at[p], r_recv.at[p], partner,
        )
        for p in range(PIECES)
    ]

    def turn(rows_at, lanes_at, p):
        for a in range(p * piece, (p + 1) * piece, 2 * LANES):
            turned[a : a + 2 * LANES, lanes_at] = recent[rows_at, a : a + 2 * LANES].T

    folded = lax.rem(mz, nz // 2) >= DIRECT

    @pl.when(folded)
    def _():
        for z in range(nz // 2):
            for d in range(1, nx):
                for c in range(FOLDING, nc):
                    away = (1 - lax.div(mz, nz // 2)) * (nz // 2) + z
                    source = (away * nx + lax.rem(mx + d, nx)) * nc + c
                    for k in range(CHUNKS):
                        land[k, source] = jnp.zeros((slab, cw), bf16)

    load_recent.wait()
    for p in range(PIECES):
        turn(own_rows, own_rows, p)
    for p in range(PIECES):
        its_recent[p].wait_recv()
        turn(its_rows, its_rows, p)
    rows = BLOCK * items
    lanes = GROUP * items
    quad = 4
    many = rank // quad
    tall = many * GROUP
    units = BLOCK // GROUP
    blocks = n * examples // BLOCK // HALVES
    lift = onehot(
        (rank * GROUP, pair_lanes),
        lambda r, c: c == rank + quad * lax.div(lax.rem(r, tall), GROUP) + lax.div(r, tall),
    )
    twice = onehot((pair_lanes, 2 * rank), lambda r, c: r == lax.rem(c, rank))
    same = onehot((tall, lanes), lambda r, c: lax.rem(r, GROUP) == lax.div(c, items))
    left_lanes = where((rows, 2 * rank), lambda r, c: c < rank)

    def arrived(source):
        @pl.when(me != source)
        def _():
            pltpu.make_async_remote_copy(
                src_ref=other, dst_ref=fac.at[source], send_sem=f_send.at[0],
                recv_sem=f_recv.at[source], device_id={"row": partner}, device_id_type=MESH,
            ).wait_recv()

    def build(b):
        every = fac[pl.ds(b * (BLOCK // examples), BLOCK // examples)].reshape(rows, pair_lanes)
        lifted = lax.dot_general(
            lift, every, (((1,), (1,)), ((), ())), preferred_element_type=f32
        ).astype(bf16)
        right = jnp.dot(every, twice, preferred_element_type=f32)
        first = jnp.where(left_lanes, right, 0.0).astype(bf16)
        second = jnp.where(left_lanes, 0.0, right).astype(bf16)
        outer = []
        for u in range(units):
            of = slice(u * lanes, (u + 1) * lanes)
            four = [lifted[i * tall : (i + 1) * tall, of] * same for i in range(quad)]
            outer.append(
                jnp.dot(
                    jnp.concatenate(
                        [jnp.concatenate(four[:2], axis=1), jnp.concatenate(four[2:], axis=1)], axis=0
                    ),
                    jnp.concatenate([first[of], second[of]], axis=0),
                    preferred_element_type=f32,
                )
            )
        pieces = []
        for a in range(many):
            for side in range(2):
                at = side * tall + a * GROUP
                pieces.append(jnp.concatenate([o[at : at + GROUP] for o in outer], axis=0))
        return (jnp.concatenate(pieces, axis=1) * (1.0 / math.sqrt(items))).astype(bf16)

    def each_block(half_at, body):
        if blocks == 1:
            body(half_at)
        else:
            lax.fori_loop(half_at * blocks, (half_at + 1) * blocks, lambda b, c: (body(b), c)[1], 0)

    at = lambda b: pl.ds(pl.multiple_of(b * BLOCK, BLOCK), BLOCK)

    def partial(b):
        mysim[at(b)] = jnp.dot(build(b), turned[...], preferred_element_type=f32)

    upper = lax.div(mz, nz // 2)
    turns = [1 - upper, upper]
    swaps = []
    for stage, h in enumerate(turns):
        for i in range(n // HALVES):
            arrived(h * (n // HALVES) + i)
        each_block(h, partial)
        of = pl.ds(pl.multiple_of(h * blocks * BLOCK, blocks * BLOCK), blocks * BLOCK)
        swaps.append(start(mysim.at[of], itssim.at[of], s_send.at[stage], s_recv.at[stage], partner))

    def term(b, k):
        weights = jnp.tanh((mysim[at(b)] + itssim[at(b)]) * (1.0 / math.sqrt(width))).astype(bf16)
        for g in range(GROUP):
            lo = g * gw + k * cw
            got = jnp.dot(weights, recent[:, lo : lo + cw], preferred_element_type=f32)
            for j in range(cw // LANES):
                tf[k, j, pl.ds(b * BLOCK * GROUP + g, BLOCK, stride=GROUP), :] = got[
                    :, j * LANES : (j + 1) * LANES
                ]
        here = pl.ds(pl.multiple_of(b * BLOCK * GROUP, BLOCK * GROUP), BLOCK * GROUP)
        for j in range(cw // LANES):
            tb.at[k].reshape(n * slab, cw)[here, j * LANES : (j + 1) * LANES] = tf[k, j, here].astype(bf16)

    def remote(src, dst, ss, rs, to):
        return pltpu.make_async_remote_copy(
            src_ref=src, dst_ref=dst, send_sem=ss, recv_sem=rs,
            device_id={"row": to}, device_id_type=MESH,
        )

    spots = [(z, x, (c + x) % nc) for x in range(nx) for z in range(nz // 2) for c in range(nc)]

    hz = nz // 2
    others = hz - DIRECT
    first = (1 - upper) * hz + DIRECT
    folds = mc >= FOLDING

    def hand(k, stage, z, x, c, wait=False):
        z_to = turns[stage] * hz + z
        to = (z_to * nx + x) * nc + c
        if stage:
            leaves = me != to
        else:
            leaves = jnp.logical_not(folds) if z >= DIRECT else None

        def go():
            copy = remote(
                tb.at[k, z_to, x, c], land.at[k, me], m_send.at[k, to], m_recv.at[k, me], to
            )
            copy.wait_send() if wait else copy.start()

        go() if leaves is None else pl.when(leaves)(go)

    def sideways(k, d):
        x = lax.rem(mx + d, nx)
        return remote(
            tb.at[k, pl.ds(first, others), x], xland.at[k, d - 1], x_send.at[k, d - 1],
            x_recv.at[k, d - 1], (mz * nx + x) * nc + mc,
        )

    def onward(k, d, c):
        to = ((first + d) * nx + mx) * nc + c
        return remote(xb.at[k, d, c], land.at[k, me], m_send.at[k, to], m_recv.at[k, me], to)

    def landed(k, source):
        remote(
            tb.at[k, 0, 0, 0], land.at[k, source], m_send.at[k, 0], m_recv.at[k, source], partner
        ).wait_recv()

    for stage, h in enumerate(turns):
        swaps[stage].wait_recv()
        for k in range(CHUNKS):
            each_block(h, functools.partial(term, k=k))
            if stage == 0:

                @pl.when(folds)
                def _():
                    for d in range(1, nx):
                        sideways(k, d).start()

            else:
                land[k, me] = tb[k, mz, mx, mc]
            for spot in spots:
                hand(k, stage, *spot)

    @pl.when(folds)
    def _():
        for k in range(CHUNKS):
            total = tb[k, pl.ds(first, others), mx].astype(f32)
            for d in range(1, nx):
                sideways(k, d).wait_recv()
                total = total + xland[k, d - 1].astype(f32)
            xb[k] = total.astype(bf16)
            for d in range(others):
                for c in range(nc):
                    onward(k, d, c).start()

    for copy in sent:
        copy.wait_send()
    for k in range(CHUNKS):
        for spot in spots:
            hand(k, FIRSTW, *spot, wait=True)

    for k in range(CHUNKS):
        for z, x, c in [(z, x, c) for z in range(nz) for x in range(nx) for c in range(nc)]:
            source = (z * nx + x) * nc + c
            comes = me != source
            if c >= FOLDING:
                comes = comes & jnp.logical_not((upper != z // hz) & folded & (mx != x))

            @pl.when(comes)
            def _():
                landed(k, source)
        totals = []
        for c in range(nc):
            total = land[k, c].astype(f32)
            for q in range(1, nz * nx):
                total = total + land[k, q * nc + c].astype(f32)
            totals.append(total)
        rows_out = [
            t[e * GROUP : (e + 1) * GROUP] for e in range(examples) for t in totals
        ]
        out_ref[:, k * cw : (k + 1) * cw] = (
            jnp.concatenate(rows_out, axis=0) * (1.0 / math.sqrt(total_recent))
        ).astype(bf16)

    for k in range(CHUNKS):
        for spot in spots:
            hand(k, 1 - FIRSTW, *spot, wait=True)

    @pl.when(folds)
    def _():
        for k in range(CHUNKS):
            for d in range(1, nx):
                sideways(k, d).wait_send()
            for d in range(others):
                for c in range(nc):
                    onward(k, d, c).wait_send()


def per_device(dims, late_grads, projections, recent_sketches):
    nz, nx, nc = dims
    local_rows, items, kinds, width_in = late_grads.shape
    rank = projections.shape[1] // 4
    local_recent, width = recent_sketches.shape
    n = nz * nx * nc
    half = width // 2
    slab, cw = local_rows * GROUP, half // GROUP // CHUNKS
    every = n * local_rows
    bf16, f32 = jnp.bfloat16, jnp.float32
    dma = pltpu.SemaphoreType.DMA
    out = pl.pallas_call(
        functools.partial(kernel, dims, items, rank, local_recent * n),
        out_shape=pltpu.VMEM((2 * slab, half // GROUP), bf16),
        in_specs=[pl.BlockSpec(memory_space=pl.ANY)] * 3,
        out_specs=pl.BlockSpec(memory_space=pltpu.VMEM),
        scratch_shapes=[
            pltpu.VMEM((local_rows * items, kinds, width_in), bf16),
            pltpu.VMEM(projections.shape, bf16),
            pltpu.VMEM((nc * local_recent, half), bf16),
            pltpu.VMEM((half, nc * local_recent), bf16),
            pltpu.VMEM((n, local_rows * items, 2 * rank), bf16),
            pltpu.VMEM((local_rows * items, 2 * rank), bf16),
            pltpu.VMEM((every, nc * local_recent), f32),
            pltpu.VMEM((every, nc * local_recent), f32),
            pltpu.VMEM((CHUNKS, cw // LANES, every * GROUP, LANES), f32),
            pltpu.VMEM((CHUNKS, nz, nx, nc, slab, cw), bf16),
            pltpu.VMEM((CHUNKS, nx - 1, nz // 2 - DIRECT, nc, slab, cw), bf16),
            pltpu.VMEM((CHUNKS, nz // 2 - DIRECT, nc, slab, cw), bf16),
            pltpu.VMEM((CHUNKS, n, slab, cw), bf16),
            dma((1 + 2 * LOADS,)),
            dma((n - 1,)),
            dma((n,)),
            dma((PIECES,)),
            dma((PIECES,)),
            dma((HALVES,)),
            dma((HALVES,)),
            dma((CHUNKS, nx - 1)),
            dma((CHUNKS, nx - 1)),
            dma((CHUNKS, n)),
            dma((CHUNKS, n)),
        ],
        compiler_params=pltpu.CompilerParams(
            collective_id=0, has_side_effects=True, vmem_limit_bytes=60 * 1024 * 1024
        ),
    )(late_grads.reshape(local_rows * items, kinds, width_in), projections, recent_sketches)
    return out.reshape(local_rows, width)


def solution(mesh):
    n = mesh.shape["row"]
    nx = 4 if n >= 64 else 2
    dims = (n // (2 * nx), nx, 2)
    placed = (P(("groups", "row"), None, None, None), P(), P(("groups", "row"), None))
    return jax.shard_map(
        functools.partial(per_device, dims),
        mesh=mesh,
        in_specs=placed,
        out_specs=P(("groups", "row"), None),
        check_vma=False,
    )
```

```python
import functools
import math

import jax
import jax.numpy as jnp
from jax import lax
from jax.experimental import pallas as pl
from jax.experimental.pallas import tpu as pltpu
from jax.sharding import PartitionSpec as P

GROUP = 8
CHUNKS = 1
LOADS = 4
BLOCK = 16
HALVES = 2
PIECES = 2
DIRECT = 1
FOLDING = 1
LANES = 128
MESH = pl.DeviceIdType.MESH


def kernel(
    dims, items, rank, total_recent,
    late_hbm, proj_hbm, recent_hbm, out_ref,
    late, proj, recent, turned, fac, other, mysim, itssim, tf, tb, xland, xb, land,
    load_sem, f_send, f_recv, r_send, r_recv, s_send, s_recv, x_send, x_recv, m_send, m_recv,
):
    nz, nx, nc = dims
    n = nz * nx * nc
    local_recent = recent_hbm.shape[0]
    half = recent.shape[1]
    width = recent_hbm.shape[1]
    pairs, pair_lanes = fac.shape[1:]
    examples = pairs // items
    slab = examples * GROUP
    gw = half // GROUP
    cw = gw // CHUNKS
    bf16, f32 = jnp.bfloat16, jnp.float32
    me = lax.axis_index("row")
    mc = lax.rem(me, nc)
    mx = lax.rem(lax.div(me, nc), nx)
    mz = lax.div(me, nc * nx)
    oc = 1 - mc

    def across(z, d):
        bit = 1
        while bit <= d:
            if d & bit:
                z = z + bit - 2 * bit * lax.rem(lax.div(z, bit), 2)
            bit *= 2
        return z

    peers = []
    for dz in reversed(range(nz)):
        for dx in reversed(range(nx)):
            for dc in (1, 0):
                if dz or dx or dc:
                    z, x = across(mz, dz), lax.rem(mx + dx, nx)
                    c = oc if dc else mc
                    peers.append(((z * nx + x) * nc + c, dc))
    partner = (mz * nx + mx) * nc + oc

    barrier = pltpu.get_barrier_semaphore()
    for index, _ in peers:
        pl.semaphore_signal(barrier, inc=1, device_id={"row": index}, device_id_type=MESH)

    depth = late.shape[2] // LOADS
    load_inputs = []
    for i in range(LOADS):
        part_of = pl.ds(i * depth, depth)
        pair = (
            pltpu.make_async_copy(late_hbm.at[:, :, part_of], late.at[:, :, part_of], load_sem.at[1 + i]),
            pltpu.make_async_copy(proj_hbm.at[part_of], proj.at[part_of], load_sem.at[1 + LOADS + i]),
        )
        for copy in pair:
            copy.start()
        load_inputs.append(pair)

    own_rows = pl.ds(pl.multiple_of(mc * local_recent, local_recent), local_recent)
    its_rows = pl.ds(pl.multiple_of(oc * local_recent, local_recent), local_recent)
    own_half = pl.ds(pl.multiple_of(mc * half, half), half)
    load_recent = pltpu.make_async_copy(
        recent_hbm.at[:, own_half], recent.at[own_rows, :], load_sem.at[0]
    )
    load_recent.start()

    def where(shape, expr):
        r = lax.broadcasted_iota(jnp.int32, shape, 0)
        c = lax.broadcasted_iota(jnp.int32, shape, 1)
        return expr(r, c)

    def onehot(shape, expr):
        return jnp.where(where(shape, expr), 1.0, 0.0).astype(bf16)

    pick = onehot((pairs, 4 * pairs), lambda r, c: r == lax.shift_right_logical(c, 2))
    full = jnp.zeros((4 * pairs, 4 * rank), f32)
    for i, pair in enumerate(load_inputs):
        for copy in pair:
            copy.wait()
        rows = late[:, :, i * depth : (i + 1) * depth].reshape(4 * pairs, depth)
        full = full + jnp.dot(rows, proj[i * depth : (i + 1) * depth, :], preferred_element_type=f32)
    full = jnp.where(
        where(full.shape, lambda r, c: lax.rem(r, 4) == lax.div(c, rank)), full, 0.0
    ).astype(bf16)
    factors = jnp.dot(pick, full, preferred_element_type=f32)
    first, second = factors[:, :pair_lanes], factors[:, pair_lanes:]
    fac[me] = jnp.where(mc == 0, first, second).astype(bf16)
    other[...] = jnp.where(mc == 0, second, first).astype(bf16)

    pl.semaphore_wait(barrier, n - 1)

    sent = []

    def start(src, dst, ss, rs, to):
        copy = pltpu.make_async_remote_copy(
            src_ref=src, dst_ref=dst, send_sem=ss, recv_sem=rs,
            device_id={"row": to}, device_id_type=MESH,
        )
        copy.start()
        sent.append(copy)
        return copy

    for slot, (to, dc) in enumerate(peers):
        start(other if dc else fac.at[me], fac.at[me], f_send.at[slot], f_recv.at[me], to)
    piece = half // PIECES
    its_recent = [
        start(
            recent_hbm.at[:, pl.ds(pl.multiple_of(oc * half + p * piece, piece), piece)],
            recent.at[own_rows, p * piece : (p + 1) * piece], r_send.at[p], r_recv.at[p], partner,
        )
        for p in range(PIECES)
    ]

    def turn(rows_at, lanes_at, p):
        for a in range(p * piece, (p + 1) * piece, 2 * LANES):
            turned[a : a + 2 * LANES, lanes_at] = recent[rows_at, a : a + 2 * LANES].T

    folded = lax.rem(mz, nz // 2) >= DIRECT

    @pl.when(folded)
    def _():
        for z in range(nz // 2):
            for d in range(1, nx):
                for c in range(FOLDING, nc):
                    away = (1 - lax.div(mz, nz // 2)) * (nz // 2) + z
                    source = (away * nx + lax.rem(mx + d, nx)) * nc + c
                    for k in range(CHUNKS):
                        land[k, source] = jnp.zeros((slab, cw), bf16)

    load_recent.wait()
    for p in range(PIECES):
        turn(own_rows, own_rows, p)
    for p in range(PIECES):
        its_recent[p].wait_recv()
        turn(its_rows, its_rows, p)
    rows = BLOCK * items
    lanes = GROUP * items
    quad = 4
    many = rank // quad
    tall = many * GROUP
    units = BLOCK // GROUP
    blocks = n * examples // BLOCK // HALVES
    lift = onehot(
        (rank * GROUP, pair_lanes),
        lambda r, c: c == rank + quad * lax.div(lax.rem(r, tall), GROUP) + lax.div(r, tall),
    )
    twice = onehot((pair_lanes, 2 * rank), lambda r, c: r == lax.rem(c, rank))
    same = onehot((tall, lanes), lambda r, c: lax.rem(r, GROUP) == lax.div(c, items))
    left_lanes = where((rows, 2 * rank), lambda r, c: c < rank)

    def arrived(source):
        @pl.when(me != source)
        def _():
            pltpu.make_async_remote_copy(
                src_ref=other, dst_ref=fac.at[source], send_sem=f_send.at[0],
                recv_sem=f_recv.at[source], device_id={"row": partner}, device_id_type=MESH,
            ).wait_recv()

    def build(b):
        every = fac[pl.ds(b * (BLOCK // examples), BLOCK // examples)].reshape(rows, pair_lanes)
        lifted = lax.dot_general(
            lift, every, (((1,), (1,)), ((), ())), preferred_element_type=f32
        ).astype(bf16)
        right = jnp.dot(every, twice, preferred_element_type=f32)
        first = jnp.where(left_lanes, right, 0.0).astype(bf16)
        second = jnp.where(left_lanes, 0.0, right).astype(bf16)
        outer = []
        for u in range(units):
            of = slice(u * lanes, (u + 1) * lanes)
            four = [lifted[i * tall : (i + 1) * tall, of] * same for i in range(quad)]
            outer.append(
                jnp.dot(
                    jnp.concatenate(
                        [jnp.concatenate(four[:2], axis=1), jnp.concatenate(four[2:], axis=1)], axis=0
                    ),
                    jnp.concatenate([first[of], second[of]], axis=0),
                    preferred_element_type=f32,
                )
            )
        pieces = []
        for a in range(many):
            for side in range(2):
                at = side * tall + a * GROUP
                pieces.append(jnp.concatenate([o[at : at + GROUP] for o in outer], axis=0))
        return (jnp.concatenate(pieces, axis=1) * (1.0 / math.sqrt(items))).astype(bf16)

    def each_block(half_at, body):
        if blocks == 1:
            body(half_at)
        else:
            lax.fori_loop(half_at * blocks, (half_at + 1) * blocks, lambda b, c: (body(b), c)[1], 0)

    at = lambda b: pl.ds(pl.multiple_of(b * BLOCK, BLOCK), BLOCK)

    def partial(b):
        mysim[at(b)] = jnp.dot(build(b), turned[...], preferred_element_type=f32)

    upper = lax.div(mz, nz // 2)
    turns = [1 - upper, upper]
    swaps = []
    for stage, h in enumerate(turns):
        for i in range(n // HALVES):
            arrived(h * (n // HALVES) + i)
        each_block(h, partial)
        of = pl.ds(pl.multiple_of(h * blocks * BLOCK, blocks * BLOCK), blocks * BLOCK)
        swaps.append(start(mysim.at[of], itssim.at[of], s_send.at[stage], s_recv.at[stage], partner))

    def term(b, k):
        weights = jnp.tanh((mysim[at(b)] + itssim[at(b)]) * (1.0 / math.sqrt(width))).astype(bf16)
        for g in range(GROUP):
            lo = g * gw + k * cw
            got = jnp.dot(weights, recent[:, lo : lo + cw], preferred_element_type=f32)
            for j in range(cw // LANES):
                tf[k, j, pl.ds(b * BLOCK * GROUP + g, BLOCK, stride=GROUP), :] = got[
                    :, j * LANES : (j + 1) * LANES
                ]
        here = pl.ds(pl.multiple_of(b * BLOCK * GROUP, BLOCK * GROUP), BLOCK * GROUP)
        for j in range(cw // LANES):
            tb.at[k].reshape(n * slab, cw)[here, j * LANES : (j + 1) * LANES] = tf[k, j, here].astype(bf16)

    def remote(src, dst, ss, rs, to):
        return pltpu.make_async_remote_copy(
            src_ref=src, dst_ref=dst, send_sem=ss, recv_sem=rs,
            device_id={"row": to}, device_id_type=MESH,
        )

    spots = [(z, x, (c + x) % nc) for x in range(nx) for z in range(nz // 2) for c in range(nc)]

    hz = nz // 2
    others = hz - DIRECT
    first = (1 - upper) * hz + DIRECT
    folds = mc >= FOLDING

    def hand(k, stage, z, x, c, wait=False):
        z_to = turns[stage] * hz + z
        to = (z_to * nx + x) * nc + c
        if stage:
            leaves = me != to
        else:
            leaves = jnp.logical_not(folds) if z >= DIRECT else None

        def go():
            copy = remote(
                tb.at[k, z_to, x, c], land.at[k, me], m_send.at[k, to], m_recv.at[k, me], to
            )
            copy.wait_send() if wait else copy.start()

        go() if leaves is None else pl.when(leaves)(go)

    def sideways(k, d):
        x = lax.rem(mx + d, nx)
        return remote(
            tb.at[k, pl.ds(first, others), x], xland.at[k, d - 1], x_send.at[k, d - 1],
            x_recv.at[k, d - 1], (mz * nx + x) * nc + mc,
        )

    def onward(k, d, c):
        to = ((first + d) * nx + mx) * nc + c
        return remote(xb.at[k, d, c], land.at[k, me], m_send.at[k, to], m_recv.at[k, me], to)

    def landed(k, source):
        remote(
            tb.at[k, 0, 0, 0], land.at[k, source], m_send.at[k, 0], m_recv.at[k, source], partner
        ).wait_recv()

    for stage, h in enumerate(turns):
        swaps[stage].wait_recv()
        for k in range(CHUNKS):
            each_block(h, functools.partial(term, k=k))
            if stage == 0:

                @pl.when(folds)
                def _():
                    for d in range(1, nx):
                        sideways(k, d).start()

            else:
                land[k, me] = tb[k, mz, mx, mc]
            for spot in spots:
                hand(k, stage, *spot)

    @pl.when(folds)
    def _():
        for k in range(CHUNKS):
            total = tb[k, pl.ds(first, others), mx].astype(f32)
            for d in range(1, nx):
                sideways(k, d).wait_recv()
                total = total + xland[k, d - 1].astype(f32)
            xb[k] = total.astype(bf16)
            for d in range(others):
                for c in range(nc):
                    onward(k, d, c).start()

    for copy in sent:
        copy.wait_send()
    for k in range(CHUNKS):
        for spot in spots:
            hand(k, 0, *spot, wait=True)

    for k in range(CHUNKS):
        for spot in spots:
            hand(k, 1, *spot, wait=True)

    @pl.when(folds)
    def _():
        for k in range(CHUNKS):
            for d in range(1, nx):
                sideways(k, d).wait_send()
            for d in range(others):
                for c in range(nc):
                    onward(k, d, c).wait_send()

    for k in range(CHUNKS):
        for z, x, c in [(z, x, c) for z in range(nz) for x in range(nx) for c in range(nc)]:
            source = (z * nx + x) * nc + c
            comes = me != source
            if c >= FOLDING:
                comes = comes & jnp.logical_not((upper != z // hz) & folded & (mx != x))

            @pl.when(comes)
            def _():
                landed(k, source)
        totals = []
        for c in range(nc):
            total = land[k, c].astype(f32)
            for q in range(1, nz * nx):
                total = total + land[k, q * nc + c].astype(f32)
            totals.append(total)
        rows_out = [
            t[e * GROUP : (e + 1) * GROUP] for e in range(examples) for t in totals
        ]
        out_ref[:, k * cw : (k + 1) * cw] = (
            jnp.concatenate(rows_out, axis=0) * (1.0 / math.sqrt(total_recent))
        ).astype(bf16)


def per_device(dims, late_grads, projections, recent_sketches):
    nz, nx, nc = dims
    local_rows, items, kinds, width_in = late_grads.shape
    rank = projections.shape[1] // 4
    local_recent, width = recent_sketches.shape
    n = nz * nx * nc
    half = width // 2
    slab, cw = local_rows * GROUP, half // GROUP // CHUNKS
    every = n * local_rows
    bf16, f32 = jnp.bfloat16, jnp.float32
    dma = pltpu.SemaphoreType.DMA
    out = pl.pallas_call(
        functools.partial(kernel, dims, items, rank, local_recent * n),
        out_shape=pltpu.VMEM((2 * slab, half // GROUP), bf16),
        in_specs=[pl.BlockSpec(memory_space=pl.ANY)] * 3,
        out_specs=pl.BlockSpec(memory_space=pltpu.VMEM),
        scratch_shapes=[
            pltpu.VMEM((local_rows * items, kinds, width_in), bf16),
            pltpu.VMEM(projections.shape, bf16),
            pltpu.VMEM((nc * local_recent, half), bf16),
            pltpu.VMEM((half, nc * local_recent), bf16),
            pltpu.VMEM((n, local_rows * items, 2 * rank), bf16),
            pltpu.VMEM((local_rows * items, 2 * rank), bf16),
            pltpu.VMEM((every, nc * local_recent), f32),
            pltpu.VMEM((every, nc * local_recent), f32),
            pltpu.VMEM((CHUNKS, cw // LANES, (every + 1) * GROUP, LANES), f32),
            pltpu.VMEM((CHUNKS, nz, nx, nc, slab, cw), bf16),
            pltpu.VMEM((CHUNKS, nx - 1, nz // 2 - DIRECT, nc, slab, cw), bf16),
            pltpu.VMEM((CHUNKS, nz // 2 - DIRECT, nc, slab, cw), bf16),
            pltpu.VMEM((CHUNKS, n, slab, cw), bf16),
            dma((1 + 2 * LOADS,)),
            dma((n - 1,)),
            dma((n,)),
            dma((PIECES,)),
            dma((PIECES,)),
            dma((HALVES,)),
            dma((HALVES,)),
            dma((CHUNKS, nx - 1)),
            dma((CHUNKS, nx - 1)),
            dma((CHUNKS, n)),
            dma((CHUNKS, n)),
        ],
        compiler_params=pltpu.CompilerParams(
            collective_id=0, has_side_effects=True, vmem_limit_bytes=60 * 1024 * 1024
        ),
    )(late_grads.reshape(local_rows * items, kinds, width_in), projections, recent_sketches)
    return out.reshape(local_rows, width)


def solution(mesh):
    n = mesh.shape["row"]
    nx = 4 if n >= 64 else 2
    dims = (n // (2 * nx), nx, 2)
    placed = (P(("groups", "row"), None, None, None), P(), P(("groups", "row"), None))
    return jax.shard_map(
        functools.partial(per_device, dims),
        mesh=mesh,
        in_specs=placed,
        out_specs=P(("groups", "row"), None),
        check_vma=False,
    )
```

```python
import functools
import math

import jax
import jax.numpy as jnp
from jax import lax
from jax.experimental import pallas as pl
from jax.experimental.pallas import tpu as pltpu
from jax.sharding import PartitionSpec as P

GROUP = 8
CHUNKS = 1
LOADS = 4
BLOCK = 16
HALVES = 2
PIECES = 2
DIRECT = 1
FOLDING = 1
LANES = 128
MESH = pl.DeviceIdType.MESH


def kernel(
    dims, items, rank, total_recent,
    late_hbm, proj_hbm, recent_hbm, out_ref,
    late, proj, recent, turned, fac, other, mysim, itssim, tf, tb, xland, xb, land,
    load_sem, f_send, f_recv, r_send, r_recv, s_send, s_recv, x_send, x_recv, m_send, m_recv,
):
    nz, nx, nc = dims
    n = nz * nx * nc
    local_recent = recent_hbm.shape[0]
    half = recent.shape[1]
    width = recent_hbm.shape[1]
    pairs, pair_lanes = fac.shape[1:]
    examples = pairs // items
    slab = examples * GROUP
    gw = half // GROUP
    cw = gw // CHUNKS
    bf16, f32 = jnp.bfloat16, jnp.float32
    me = lax.axis_index("row")
    mc = lax.rem(me, nc)
    mx = lax.rem(lax.div(me, nc), nx)
    mz = lax.div(me, nc * nx)
    oc = 1 - mc

    def across(z, d):
        bit = 1
        while bit <= d:
            if d & bit:
                z = z + bit - 2 * bit * lax.rem(lax.div(z, bit), 2)
            bit *= 2
        return z

    peers = []
    for dz in reversed(range(nz)):
        for dx in reversed(range(nx)):
            for dc in (1, 0):
                if dz or dx or dc:
                    z, x = across(mz, dz), lax.rem(mx + dx, nx)
                    c = oc if dc else mc
                    peers.append(((z * nx + x) * nc + c, dc))
    partner = (mz * nx + mx) * nc + oc

    barrier = pltpu.get_barrier_semaphore()
    for index, _ in peers:
        pl.semaphore_signal(barrier, inc=1, device_id={"row": index}, device_id_type=MESH)

    depth = late.shape[2] // LOADS
    load_inputs = []
    for i in range(LOADS):
        part_of = pl.ds(i * depth, depth)
        pair = (
            pltpu.make_async_copy(late_hbm.at[:, :, part_of], late.at[:, :, part_of], load_sem.at[1 + i]),
            pltpu.make_async_copy(proj_hbm.at[part_of], proj.at[part_of], load_sem.at[1 + LOADS + i]),
        )
        for copy in pair:
            copy.start()
        load_inputs.append(pair)

    own_rows = pl.ds(pl.multiple_of(mc * local_recent, local_recent), local_recent)
    its_rows = pl.ds(pl.multiple_of(oc * local_recent, local_recent), local_recent)
    own_half = pl.ds(pl.multiple_of(mc * half, half), half)
    load_recent = pltpu.make_async_copy(
        recent_hbm.at[:, own_half], recent.at[own_rows, :], load_sem.at[0]
    )
    load_recent.start()

    def where(shape, expr):
        r = lax.broadcasted_iota(jnp.int32, shape, 0)
        c = lax.broadcasted_iota(jnp.int32, shape, 1)
        return expr(r, c)

    def onehot(shape, expr):
        return jnp.where(where(shape, expr), 1.0, 0.0).astype(bf16)

    pick = onehot((pairs, 4 * pairs), lambda r, c: r == lax.shift_right_logical(c, 2))
    full = jnp.zeros((4 * pairs, 4 * rank), f32)
    for i, pair in enumerate(load_inputs):
        for copy in pair:
            copy.wait()
        rows = late[:, :, i * depth : (i + 1) * depth].reshape(4 * pairs, depth)
        full = full + jnp.dot(rows, proj[i * depth : (i + 1) * depth, :], preferred_element_type=f32)
    full = jnp.where(
        where(full.shape, lambda r, c: lax.rem(r, 4) == lax.div(c, rank)), full, 0.0
    ).astype(bf16)
    factors = jnp.dot(pick, full, preferred_element_type=f32)
    first, second = factors[:, :pair_lanes], factors[:, pair_lanes:]
    fac[me] = jnp.where(mc == 0, first, second).astype(bf16)
    other[...] = jnp.where(mc == 0, second, first).astype(bf16)

    pl.semaphore_wait(barrier, n - 1)

    sent = []

    def start(src, dst, ss, rs, to):
        copy = pltpu.make_async_remote_copy(
            src_ref=src, dst_ref=dst, send_sem=ss, recv_sem=rs,
            device_id={"row": to}, device_id_type=MESH,
        )
        copy.start()
        sent.append(copy)
        return copy

    for slot, (to, dc) in enumerate(peers):
        start(other if dc else fac.at[me], fac.at[me], f_send.at[slot], f_recv.at[me], to)
    piece = half // PIECES
    its_recent = [
        start(
            recent_hbm.at[:, pl.ds(pl.multiple_of(oc * half + p * piece, piece), piece)],
            recent.at[own_rows, p * piece : (p + 1) * piece], r_send.at[p], r_recv.at[p], partner,
        )
        for p in range(PIECES)
    ]

    def turn(rows_at, lanes_at, p):
        for a in range(p * piece, (p + 1) * piece, 2 * LANES):
            turned[a : a + 2 * LANES, lanes_at] = recent[rows_at, a : a + 2 * LANES].T

    folded = lax.rem(mz, nz // 2) >= DIRECT

    @pl.when(folded)
    def _():
        for z in range(nz // 2):
            for d in range(1, nx):
                for c in range(FOLDING, nc):
                    away = (1 - lax.div(mz, nz // 2)) * (nz // 2) + z
                    source = (away * nx + lax.rem(mx + d, nx)) * nc + c
                    for k in range(CHUNKS):
                        land[k, source] = jnp.zeros((slab, cw), bf16)

    load_recent.wait()
    for p in range(PIECES):
        turn(own_rows, own_rows, p)
    for p in range(PIECES):
        its_recent[p].wait_recv()
        turn(its_rows, its_rows, p)
    rows = BLOCK * items
    lanes = GROUP * items
    quad = 4
    many = rank // quad
    tall = many * GROUP
    units = BLOCK // GROUP
    blocks = n * examples // BLOCK // HALVES
    lift = onehot(
        (rank * GROUP, pair_lanes),
        lambda r, c: c == rank + quad * lax.div(lax.rem(r, tall), GROUP) + lax.div(r, tall),
    )
    twice = onehot((pair_lanes, 2 * rank), lambda r, c: r == lax.rem(c, rank))
    same = onehot((tall, lanes), lambda r, c: lax.rem(r, GROUP) == lax.div(c, items))
    left_lanes = where((rows, 2 * rank), lambda r, c: c < rank)

    def arrived(source):
        @pl.when(me != source)
        def _():
            pltpu.make_async_remote_copy(
                src_ref=other, dst_ref=fac.at[source], send_sem=f_send.at[0],
                recv_sem=f_recv.at[source], device_id={"row": partner}, device_id_type=MESH,
            ).wait_recv()

    def build(b):
        every = fac[pl.ds(b * (BLOCK // examples), BLOCK // examples)].reshape(rows, pair_lanes)
        lifted = lax.dot_general(
            lift, every, (((1,), (1,)), ((), ())), preferred_element_type=f32
        ).astype(bf16)
        right = jnp.dot(every, twice, preferred_element_type=f32)
        first = jnp.where(left_lanes, right, 0.0).astype(bf16)
        second = jnp.where(left_lanes, 0.0, right).astype(bf16)
        outer = []
        for u in range(units):
            of = slice(u * lanes, (u + 1) * lanes)
            four = [lifted[i * tall : (i + 1) * tall, of] * same for i in range(quad)]
            outer.append(
                jnp.dot(
                    jnp.concatenate(
                        [jnp.concatenate(four[:2], axis=1), jnp.concatenate(four[2:], axis=1)], axis=0
                    ),
                    jnp.concatenate([first[of], second[of]], axis=0),
                    preferred_element_type=f32,
                )
            )
        pieces = []
        for a in range(many):
            for side in range(2):
                at = side * tall + a * GROUP
                pieces.append(jnp.concatenate([o[at : at + GROUP] for o in outer], axis=0))
        return (jnp.concatenate(pieces, axis=1) * (1.0 / math.sqrt(items))).astype(bf16)

    def each_block(half_at, body):
        if blocks == 1:
            body(half_at)
        else:
            lax.fori_loop(half_at * blocks, (half_at + 1) * blocks, lambda b, c: (body(b), c)[1], 0)

    at = lambda b: pl.ds(pl.multiple_of(b * BLOCK, BLOCK), BLOCK)

    def partial(b):
        mysim[at(b)] = jnp.dot(build(b), turned[...], preferred_element_type=f32)

    upper = lax.div(mz, nz // 2)
    turns = [1 - upper, upper]
    swaps = []
    for stage, h in enumerate(turns):
        for i in range(n // HALVES):
            arrived(h * (n // HALVES) + i)
        each_block(h, partial)
        of = pl.ds(pl.multiple_of(h * blocks * BLOCK, blocks * BLOCK), blocks * BLOCK)
        swaps.append(start(mysim.at[of], itssim.at[of], s_send.at[stage], s_recv.at[stage], partner))

    def term(b, k):
        weights = jnp.tanh((mysim[at(b)] + itssim[at(b)]) * (1.0 / math.sqrt(width))).astype(bf16)
        for g in range(GROUP):
            lo = g * gw + k * cw
            got = jnp.dot(weights, recent[:, lo : lo + cw], preferred_element_type=f32)
            for j in range(cw // LANES):
                tf[k, j, pl.ds(b * BLOCK * GROUP + g, BLOCK, stride=GROUP), :] = got[
                    :, j * LANES : (j + 1) * LANES
                ]
        here = pl.ds(pl.multiple_of(b * BLOCK * GROUP, BLOCK * GROUP), BLOCK * GROUP)
        for j in range(cw // LANES):
            tb.at[k].reshape(n * slab, cw)[here, j * LANES : (j + 1) * LANES] = tf[k, j, here].astype(bf16)

    def remote(src, dst, ss, rs, to):
        return pltpu.make_async_remote_copy(
            src_ref=src, dst_ref=dst, send_sem=ss, recv_sem=rs,
            device_id={"row": to}, device_id_type=MESH,
        )

    spots = [(z, x, (c + x) % nc) for x in range(nx) for z in range(nz // 2) for c in range(nc)]

    hz = nz // 2
    others = hz - DIRECT
    first = (1 - upper) * hz + DIRECT
    folds = mc >= FOLDING

    def hand(k, stage, z, x, c, wait=False):
        z_to = turns[stage] * hz + z
        to = (z_to * nx + x) * nc + c
        if stage:
            leaves = me != to
        else:
            leaves = jnp.logical_not(folds) if z >= DIRECT else None

        def go():
            copy = remote(
                tb.at[k, z_to, x, c], land.at[k, me], m_send.at[k, to], m_recv.at[k, me], to
            )
            copy.wait_send() if wait else copy.start()

        go() if leaves is None else pl.when(leaves)(go)

    def sideways(k, d):
        x = lax.rem(mx + d, nx)
        return remote(
            tb.at[k, pl.ds(first, others), x], xland.at[k, d - 1], x_send.at[k, d - 1],
            x_recv.at[k, d - 1], (mz * nx + x) * nc + mc,
        )

    def onward(k, d, c):
        to = ((first + d) * nx + mx) * nc + c
        return remote(xb.at[k, d, c], land.at[k, me], m_send.at[k, to], m_recv.at[k, me], to)

    def landed(k, source):
        remote(
            tb.at[k, 0, 0, 0], land.at[k, source], m_send.at[k, 0], m_recv.at[k, source], partner
        ).wait_recv()

    for stage, h in enumerate(turns):
        swaps[stage].wait_recv()
        for k in range(CHUNKS):
            each_block(h, functools.partial(term, k=k))
            if stage == 0:

                @pl.when(folds)
                def _():
                    for d in range(1, nx):
                        sideways(k, d).start()

            else:
                land[k, me] = tb[k, mz, mx, mc]
            for spot in spots:
                hand(k, stage, *spot)

    @pl.when(folds)
    def _():
        for k in range(CHUNKS):
            total = tb[k, pl.ds(first, others), mx].astype(f32)
            for d in range(1, nx):
                sideways(k, d).wait_recv()
                total = total + xland[k, d - 1].astype(f32)
            xb[k] = total.astype(bf16)
            for d in range(others):
                for c in range(nc):
                    onward(k, d, c).start()

    for copy in sent:
        copy.wait_send()
    for k in range(CHUNKS):
        for spot in spots:
            hand(k, 0, *spot, wait=True)

    for k in range(CHUNKS):
        for spot in spots:
            hand(k, 1, *spot, wait=True)

    @pl.when(folds)
    def _():
        for k in range(CHUNKS):
            for d in range(1, nx):
                sideways(k, d).wait_send()
            for d in range(others):
                for c in range(nc):
                    onward(k, d, c).wait_send()

    for k in range(CHUNKS):
        totals = [jnp.zeros((slab, cw), f32)] * nc
        for h in (upper, 1 - upper):
            for z in range(hz):
                for x in range(nx):
                    for c in range(nc):
                        source = ((h * hz + z) * nx + x) * nc + c
                        comes = me != source
                        if c >= FOLDING:
                            comes = comes & jnp.logical_not((h != upper) & folded & (mx != x))

                        @pl.when(comes)
                        def _():
                            landed(k, source)

            for c in range(nc):
                for q in range(hz * nx):
                    totals[c] = totals[c] + land[k, (h * hz * nx + q) * nc + c].astype(f32)
        rows_out = [
            t[e * GROUP : (e + 1) * GROUP] for e in range(examples) for t in totals
        ]
        out_ref[:, k * cw : (k + 1) * cw] = (
            jnp.concatenate(rows_out, axis=0) * (1.0 / math.sqrt(total_recent))
        ).astype(bf16)


def per_device(dims, late_grads, projections, recent_sketches):
    nz, nx, nc = dims
    local_rows, items, kinds, width_in = late_grads.shape
    rank = projections.shape[1] // 4
    local_recent, width = recent_sketches.shape
    n = nz * nx * nc
    half = width // 2
    slab, cw = local_rows * GROUP, half // GROUP // CHUNKS
    every = n * local_rows
    bf16, f32 = jnp.bfloat16, jnp.float32
    dma = pltpu.SemaphoreType.DMA
    out = pl.pallas_call(
        functools.partial(kernel, dims, items, rank, local_recent * n),
        out_shape=pltpu.VMEM((2 * slab, half // GROUP), bf16),
        in_specs=[pl.BlockSpec(memory_space=pl.ANY)] * 3,
        out_specs=pl.BlockSpec(memory_space=pltpu.VMEM),
        scratch_shapes=[
            pltpu.VMEM((local_rows * items, kinds, width_in), bf16),
            pltpu.VMEM(projections.shape, bf16),
            pltpu.VMEM((nc * local_recent, half), bf16),
            pltpu.VMEM((half, nc * local_recent), bf16),
            pltpu.VMEM((n, local_rows * items, 2 * rank), bf16),
            pltpu.VMEM((local_rows * items, 2 * rank), bf16),
            pltpu.VMEM((every, nc * local_recent), f32),
            pltpu.VMEM((every, nc * local_recent), f32),
            pltpu.VMEM((CHUNKS, cw // LANES, (every + 1) * GROUP, LANES), f32),
            pltpu.VMEM((CHUNKS, nz, nx, nc, slab, cw), bf16),
            pltpu.VMEM((CHUNKS, nx - 1, nz // 2 - DIRECT, nc, slab, cw), bf16),
            pltpu.VMEM((CHUNKS, nz // 2 - DIRECT, nc, slab, cw), bf16),
            pltpu.VMEM((CHUNKS, n, slab, cw), bf16),
            dma((1 + 2 * LOADS,)),
            dma((n - 1,)),
            dma((n,)),
            dma((PIECES,)),
            dma((PIECES,)),
            dma((HALVES,)),
            dma((HALVES,)),
            dma((CHUNKS, nx - 1)),
            dma((CHUNKS, nx - 1)),
            dma((CHUNKS, n)),
            dma((CHUNKS, n)),
        ],
        compiler_params=pltpu.CompilerParams(
            collective_id=0, has_side_effects=True, vmem_limit_bytes=60 * 1024 * 1024
        ),
    )(late_grads.reshape(local_rows * items, kinds, width_in), projections, recent_sketches)
    return out.reshape(local_rows, width)


def solution(mesh):
    n = mesh.shape["row"]
    nx = 4 if n >= 64 else 2
    dims = (n // (2 * nx), nx, 2)
    placed = (P(("groups", "row"), None, None, None), P(), P(("groups", "row"), None))
    return jax.shard_map(
        functools.partial(per_device, dims),
        mesh=mesh,
        in_specs=placed,
        out_specs=P(("groups", "row"), None),
        check_vma=False,
    )
```

```python
import functools
import math

import jax
import jax.numpy as jnp
from jax import lax
from jax.experimental import pallas as pl
from jax.experimental.pallas import tpu as pltpu
from jax.sharding import PartitionSpec as P

GROUP = 8
CHUNKS = 1
LOADS = 4
BLOCK = 16
HALVES = 2
PIECES = 2
DIRECT = 1
FOLDING = 1
LANES = 128
MESH = pl.DeviceIdType.MESH


def kernel(
    dims, items, rank, total_recent,
    late_hbm, proj_hbm, recent_hbm, out_ref,
    late, proj, recent, turned, fac, other, mysim, itssim, tf, tb, xland, xb, land,
    load_sem, f_send, f_recv, r_send, r_recv, s_send, s_recv, x_send, x_recv, m_send, m_recv,
):
    nz, nx, nc = dims
    n = nz * nx * nc
    local_recent = recent_hbm.shape[0]
    half = recent.shape[1]
    width = recent_hbm.shape[1]
    pairs, pair_lanes = fac.shape[1:]
    examples = pairs // items
    slab = examples * GROUP
    gw = half // GROUP
    cw = gw // CHUNKS
    bf16, f32 = jnp.bfloat16, jnp.float32
    me = lax.axis_index("row")
    mc = lax.rem(me, nc)
    mx = lax.rem(lax.div(me, nc), nx)
    mz = lax.div(me, nc * nx)
    oc = 1 - mc

    def across(z, d):
        bit = 1
        while bit <= d:
            if d & bit:
                z = z + bit - 2 * bit * lax.rem(lax.div(z, bit), 2)
            bit *= 2
        return z

    peers = []
    for dz in reversed(range(nz)):
        for dx in reversed(range(nx)):
            for dc in (1, 0):
                if dz or dx or dc:
                    z, x = across(mz, dz), lax.rem(mx + dx, nx)
                    c = oc if dc else mc
                    peers.append(((z * nx + x) * nc + c, dc))
    partner = (mz * nx + mx) * nc + oc

    barrier = pltpu.get_barrier_semaphore()
    for index, _ in peers:
        pl.semaphore_signal(barrier, inc=1, device_id={"row": index}, device_id_type=MESH)

    depth = late.shape[2] // LOADS
    load_inputs = []
    for i in range(LOADS):
        part_of = pl.ds(i * depth, depth)
        pair = (
            pltpu.make_async_copy(late_hbm.at[:, :, part_of], late.at[:, :, part_of], load_sem.at[1 + i]),
            pltpu.make_async_copy(proj_hbm.at[part_of], proj.at[part_of], load_sem.at[1 + LOADS + i]),
        )
        for copy in pair:
            copy.start()
        load_inputs.append(pair)

    own_rows = pl.ds(pl.multiple_of(mc * local_recent, local_recent), local_recent)
    its_rows = pl.ds(pl.multiple_of(oc * local_recent, local_recent), local_recent)
    own_half = pl.ds(pl.multiple_of(mc * half, half), half)
    load_recent = pltpu.make_async_copy(
        recent_hbm.at[:, own_half], recent.at[own_rows, :], load_sem.at[0]
    )
    load_recent.start()

    def where(shape, expr):
        r = lax.broadcasted_iota(jnp.int32, shape, 0)
        c = lax.broadcasted_iota(jnp.int32, shape, 1)
        return expr(r, c)

    def onehot(shape, expr):
        return jnp.where(where(shape, expr), 1.0, 0.0).astype(bf16)

    pick = onehot((pairs, 4 * pairs), lambda r, c: r == lax.shift_right_logical(c, 2))
    full = jnp.zeros((4 * pairs, 4 * rank), f32)
    for i, pair in enumerate(load_inputs):
        for copy in pair:
            copy.wait()
        rows = late[:, :, i * depth : (i + 1) * depth].reshape(4 * pairs, depth)
        full = full + jnp.dot(rows, proj[i * depth : (i + 1) * depth, :], preferred_element_type=f32)
    full = jnp.where(
        where(full.shape, lambda r, c: lax.rem(r, 4) == lax.div(c, rank)), full, 0.0
    ).astype(bf16)
    factors = jnp.dot(pick, full, preferred_element_type=f32)
    first, second = factors[:, :pair_lanes], factors[:, pair_lanes:]
    fac[me] = jnp.where(mc == 0, first, second).astype(bf16)
    other[...] = jnp.where(mc == 0, second, first).astype(bf16)

    pl.semaphore_wait(barrier, n - 1)

    sent = []

    def start(src, dst, ss, rs, to):
        copy = pltpu.make_async_remote_copy(
            src_ref=src, dst_ref=dst, send_sem=ss, recv_sem=rs,
            device_id={"row": to}, device_id_type=MESH,
        )
        copy.start()
        sent.append(copy)
        return copy

    for slot, (to, dc) in enumerate(peers):
        start(other if dc else fac.at[me], fac.at[me], f_send.at[slot], f_recv.at[me], to)
    piece = half // PIECES
    its_recent = [
        start(
            recent_hbm.at[:, pl.ds(pl.multiple_of(oc * half + p * piece, piece), piece)],
            recent.at[own_rows, p * piece : (p + 1) * piece], r_send.at[p], r_recv.at[p], partner,
        )
        for p in range(PIECES)
    ]

    def turn(rows_at, lanes_at, p):
        for a in range(p * piece, (p + 1) * piece, 2 * LANES):
            turned[a : a + 2 * LANES, lanes_at] = recent[rows_at, a : a + 2 * LANES].T

    folded = lax.rem(mz, nz // 2) >= DIRECT

    @pl.when(folded)
    def _():
        for z in range(nz // 2):
            for d in range(1, nx):
                for c in range(FOLDING, nc):
                    away = (1 - lax.div(mz, nz // 2)) * (nz // 2) + z
                    source = (away * nx + lax.rem(mx + d, nx)) * nc + c
                    for k in range(CHUNKS):
                        land[k, source] = jnp.zeros((slab, cw), bf16)

    load_recent.wait()
    for p in range(PIECES):
        turn(own_rows, own_rows, p)
    for p in range(PIECES):
        its_recent[p].wait_recv()
        turn(its_rows, its_rows, p)
    rows = BLOCK * items
    lanes = GROUP * items
    quad = 4
    many = rank // quad
    tall = many * GROUP
    units = BLOCK // GROUP
    blocks = n * examples // BLOCK // HALVES
    lift = onehot(
        (rank * GROUP, pair_lanes),
        lambda r, c: c == rank + quad * lax.div(lax.rem(r, tall), GROUP) + lax.div(r, tall),
    )
    twice = onehot((pair_lanes, 2 * rank), lambda r, c: r == lax.rem(c, rank))
    same = onehot((tall, lanes), lambda r, c: lax.rem(r, GROUP) == lax.div(c, items))
    left_lanes = where((rows, 2 * rank), lambda r, c: c < rank)

    def arrived(source):
        @pl.when(me != source)
        def _():
            pltpu.make_async_remote_copy(
                src_ref=other, dst_ref=fac.at[source], send_sem=f_send.at[0],
                recv_sem=f_recv.at[source], device_id={"row": partner}, device_id_type=MESH,
            ).wait_recv()

    def build(b):
        every = fac[pl.ds(b * (BLOCK // examples), BLOCK // examples)].reshape(rows, pair_lanes)
        lifted = lax.dot_general(
            lift, every, (((1,), (1,)), ((), ())), preferred_element_type=f32
        ).astype(bf16)
        right = jnp.dot(every, twice, preferred_element_type=f32)
        first = jnp.where(left_lanes, right, 0.0).astype(bf16)
        second = jnp.where(left_lanes, 0.0, right).astype(bf16)
        outer = []
        for u in range(units):
            of = slice(u * lanes, (u + 1) * lanes)
            four = [lifted[i * tall : (i + 1) * tall, of] * same for i in range(quad)]
            outer.append(
                jnp.dot(
                    jnp.concatenate(
                        [jnp.concatenate(four[:2], axis=1), jnp.concatenate(four[2:], axis=1)], axis=0
                    ),
                    jnp.concatenate([first[of], second[of]], axis=0),
                    preferred_element_type=f32,
                )
            )
        pieces = []
        for a in range(many):
            for side in range(2):
                at = side * tall + a * GROUP
                pieces.append(jnp.concatenate([o[at : at + GROUP] for o in outer], axis=0))
        return (jnp.concatenate(pieces, axis=1) * (1.0 / math.sqrt(items))).astype(bf16)

    def each_block(half_at, body):
        if blocks == 1:
            body(half_at)
        else:
            lax.fori_loop(half_at * blocks, (half_at + 1) * blocks, lambda b, c: (body(b), c)[1], 0)

    at = lambda b: pl.ds(pl.multiple_of(b * BLOCK, BLOCK), BLOCK)

    def partial(b):
        mysim[at(b)] = jnp.dot(build(b), turned[...], preferred_element_type=f32)

    upper = lax.div(mz, nz // 2)
    turns = [1 - upper, upper]
    swaps = []
    for stage, h in enumerate(turns):
        for i in range(n // HALVES):
            arrived(h * (n // HALVES) + i)
        each_block(h, partial)
        of = pl.ds(pl.multiple_of(h * blocks * BLOCK, blocks * BLOCK), blocks * BLOCK)
        swaps.append(start(mysim.at[of], itssim.at[of], s_send.at[stage], s_recv.at[stage], partner))

    def term(b, k):
        weights = jnp.tanh((mysim[at(b)] + itssim[at(b)]) * (1.0 / math.sqrt(width))).astype(bf16)
        for g in range(GROUP):
            lo = g * gw + k * cw
            got = jnp.dot(weights, recent[:, lo : lo + cw], preferred_element_type=f32)
            for j in range(cw // LANES):
                tf[k, j, pl.ds(b * BLOCK * GROUP + g, BLOCK, stride=GROUP), :] = got[
                    :, j * LANES : (j + 1) * LANES
                ]
        here = pl.ds(pl.multiple_of(b * BLOCK * GROUP, BLOCK * GROUP), BLOCK * GROUP)
        for j in range(cw // LANES):
            tb.at[k].reshape(n * slab, cw)[here, j * LANES : (j + 1) * LANES] = tf[k, j, here].astype(bf16)

    def remote(src, dst, ss, rs, to):
        return pltpu.make_async_remote_copy(
            src_ref=src, dst_ref=dst, send_sem=ss, recv_sem=rs,
            device_id={"row": to}, device_id_type=MESH,
        )

    spots = [(z, x, (c + x) % nc) for x in range(nx) for z in range(nz // 2) for c in range(nc)]

    hz = nz // 2
    others = hz - DIRECT
    first = (1 - upper) * hz + DIRECT
    folds = mc >= FOLDING

    def hand(k, stage, z, x, c, wait=False):
        z_to = turns[stage] * hz + z
        to = (z_to * nx + x) * nc + c
        if stage:
            leaves = me != to
        else:
            leaves = jnp.logical_not(folds) if z >= DIRECT else None

        def go():
            copy = remote(
                tb.at[k, z_to, x, c], land.at[k, me], m_send.at[k, to], m_recv.at[k, me], to
            )
            copy.wait_send() if wait else copy.start()

        go() if leaves is None else pl.when(leaves)(go)

    def sideways(k, d):
        x = lax.rem(mx + d, nx)
        return remote(
            tb.at[k, pl.ds(first, others), x], xland.at[k, d - 1], x_send.at[k, d - 1],
            x_recv.at[k, d - 1], (mz * nx + x) * nc + mc,
        )

    def onward(k, d, c):
        to = ((first + d) * nx + mx) * nc + c
        return remote(xb.at[k, d, c], land.at[k, me], m_send.at[k, to], m_recv.at[k, me], to)

    def landed(k, source):
        remote(
            tb.at[k, 0, 0, 0], land.at[k, source], m_send.at[k, 0], m_recv.at[k, source], partner
        ).wait_recv()

    for stage, h in enumerate(turns):
        swaps[stage].wait_recv()
        for k in range(CHUNKS):
            each_block(h, functools.partial(term, k=k))
            if stage:
                land[k, me] = tb[k, mz, mx, mc]
            for i, spot in enumerate(spots):
                if stage == 0 and i == nc:

                    @pl.when(folds)
                    def _():
                        for d in range(1, nx):
                            sideways(k, d).start()

                hand(k, stage, *spot)

    @pl.when(folds)
    def _():
        for k in range(CHUNKS):
            total = tb[k, pl.ds(first, others), mx].astype(f32)
            for d in range(1, nx):
                sideways(k, d).wait_recv()
                total = total + xland[k, d - 1].astype(f32)
            xb[k] = total.astype(bf16)
            for d in range(others):
                for c in range(nc):
                    onward(k, d, c).start()

    for copy in sent:
        copy.wait_send()
    for k in range(CHUNKS):
        for spot in spots:
            hand(k, 0, *spot, wait=True)

    for k in range(CHUNKS):
        for spot in spots:
            hand(k, 1, *spot, wait=True)

    @pl.when(folds)
    def _():
        for k in range(CHUNKS):
            for d in range(1, nx):
                sideways(k, d).wait_send()
            for d in range(others):
                for c in range(nc):
                    onward(k, d, c).wait_send()

    for k in range(CHUNKS):
        for z, x, c in [(z, x, c) for z in range(nz) for x in range(nx) for c in range(nc)]:
            source = (z * nx + x) * nc + c
            comes = me != source
            if c >= FOLDING:
                comes = comes & jnp.logical_not((upper != z // hz) & folded & (mx != x))

            @pl.when(comes)
            def _():
                landed(k, source)
        totals = []
        for c in range(nc):
            total = land[k, c].astype(f32)
            for q in range(1, nz * nx):
                total = total + land[k, q * nc + c].astype(f32)
            totals.append(total)
        rows_out = [
            t[e * GROUP : (e + 1) * GROUP] for e in range(examples) for t in totals
        ]
        out_ref[:, k * cw : (k + 1) * cw] = (
            jnp.concatenate(rows_out, axis=0) * (1.0 / math.sqrt(total_recent))
        ).astype(bf16)


def per_device(dims, late_grads, projections, recent_sketches):
    nz, nx, nc = dims
    local_rows, items, kinds, width_in = late_grads.shape
    rank = projections.shape[1] // 4
    local_recent, width = recent_sketches.shape
    n = nz * nx * nc
    half = width // 2
    slab, cw = local_rows * GROUP, half // GROUP // CHUNKS
    every = n * local_rows
    bf16, f32 = jnp.bfloat16, jnp.float32
    dma = pltpu.SemaphoreType.DMA
    out = pl.pallas_call(
        functools.partial(kernel, dims, items, rank, local_recent * n),
        out_shape=pltpu.VMEM((2 * slab, half // GROUP), bf16),
        in_specs=[pl.BlockSpec(memory_space=pl.ANY)] * 3,
        out_specs=pl.BlockSpec(memory_space=pltpu.VMEM),
        scratch_shapes=[
            pltpu.VMEM((local_rows * items, kinds, width_in), bf16),
            pltpu.VMEM(projections.shape, bf16),
            pltpu.VMEM((nc * local_recent, half), bf16),
            pltpu.VMEM((half, nc * local_recent), bf16),
            pltpu.VMEM((n, local_rows * items, 2 * rank), bf16),
            pltpu.VMEM((local_rows * items, 2 * rank), bf16),
            pltpu.VMEM((every, nc * local_recent), f32),
            pltpu.VMEM((every, nc * local_recent), f32),
            pltpu.VMEM((CHUNKS, cw // LANES, (every + 1) * GROUP, LANES), f32),
            pltpu.VMEM((CHUNKS, nz, nx, nc, slab, cw), bf16),
            pltpu.VMEM((CHUNKS, nx - 1, nz // 2 - DIRECT, nc, slab, cw), bf16),
            pltpu.VMEM((CHUNKS, nz // 2 - DIRECT, nc, slab, cw), bf16),
            pltpu.VMEM((CHUNKS, n, slab, cw), bf16),
            dma((1 + 2 * LOADS,)),
            dma((n - 1,)),
            dma((n,)),
            dma((PIECES,)),
            dma((PIECES,)),
            dma((HALVES,)),
            dma((HALVES,)),
            dma((CHUNKS, nx - 1)),
            dma((CHUNKS, nx - 1)),
            dma((CHUNKS, n)),
            dma((CHUNKS, n)),
        ],
        compiler_params=pltpu.CompilerParams(
            collective_id=0, has_side_effects=True, vmem_limit_bytes=60 * 1024 * 1024
        ),
    )(late_grads.reshape(local_rows * items, kinds, width_in), projections, recent_sketches)
    return out.reshape(local_rows, width)


def solution(mesh):
    n = mesh.shape["row"]
    nx = 4 if n >= 64 else 2
    dims = (n // (2 * nx), nx, 2)
    placed = (P(("groups", "row"), None, None, None), P(), P(("groups", "row"), None))
    return jax.shard_map(
        functools.partial(per_device, dims),
        mesh=mesh,
        in_specs=placed,
        out_specs=P(("groups", "row"), None),
        check_vma=False,
    )
```
